128 devices in a mesh: clip: 8 (over x, core), tok: 16 (over y, z).
Axes of the slice: x: 4, y: 4, z: 4, core: 2. Of those that a mesh axis runs over, the one named last changes fastest.
Arguments:
- tokens: bfloat16 [65536, 1024], P(('clip', 'tok')), may hold values from -80 to 80
- slot_keys: bfloat16 [1024, 1024], replicated, may hold values from -64 to 64
- w_in: bfloat16 [16, 1024, 4096], P('tok', None, 'clip'), may hold values from -0.1875 to 0.1875
- w_back: bfloat16 [16, 4096, 1024], P('tok', 'clip'), may hold values from -0.09375 to 0.09375
- w_proj: bfloat16 [1024, 512], replicated, may hold values from -0.1875 to 0.1875
- dec_source: int32 [8, 4096], P('clip'), may hold values from 0 to 8192, as said below
- mask_token: bfloat16 [512], replicated, may hold values from -80 to 80
- w_qkv: bfloat16 [512, 1536], replicated, may hold values from -8 to 8
- w_out: bfloat16 [512, 512], replicated, may hold values from -9 to 9
Outputs:
- decoded: bfloat16 [32768, 512], P(('clip', 'tok'))
The draws below stay inside these ranges and needn't reach their ends.
Inputs may be any that keep to these rules, and one draw needn't show every extreme that they name: `dec_source`: within a clip no visible index appears twice. For each aligned block of 256 decoder positions and each aligned block of 512 visible tokens, at most 16 positions of the first show tokens of the second, and some pair of blocks reaches 16 in every clip.
All inputs are finite; a program needn't handle non-finite values.
Results may differ from the reference program's by a relative error of at most 0.025.
Values may be sent and summed in bfloat16 or wider, within the bound.
A program may use at most 64 MiB of HBM per device.

```python
import math
import jax
import jax.numpy as jnp
from jax import lax

D = 1024
HID = 4096
SLOTS_E = 64
DD = 512
HEADS = 16
VIS_DEV = 512
EXPERTS = 16
SLOTS = 1024
HD = 32
CLIPS = 8
VIS = 8192
DEC_DEV = 256
DEC = 4096
CAP = 16


def draw_tokens(key, part):
    base = jax.random.normal(jax.random.fold_in(key, 1), (CLIPS * VIS, D), jnp.float32)
    return base.astype(jnp.bfloat16)


def draw_slot_keys(key, part):
    return (jax.random.normal(jax.random.fold_in(key, 21), (D, SLOTS), jnp.float32) * (2.5 / math.sqrt(D))).astype(jnp.bfloat16)


def draw_mask_token(key, part):
    noise = jax.random.normal(jax.random.fold_in(key, 31), (DD,), jnp.float32)
    return noise.astype(jnp.bfloat16)


def draw_w_qkv(key, part):
    base = jax.random.normal(jax.random.fold_in(key, 41), (DD, 3 * DD), jnp.float32) / math.sqrt(DD)
    return base.astype(jnp.bfloat16)


def draw_dec_source(key, part):
    groups = DEC // DEC_DEV

    def one_clip(clip_key):
        salts = [jax.random.fold_in(clip_key, index) for index in range(6)]
        levels = jax.random.randint(salts[0], (groups,), 0, 4)
        ceiling = jnp.maximum(CAP // 2 ** levels, 1)
        counts = ceiling[None, :] - jax.random.randint(salts[1], (groups, groups), 0, ceiling[None, :] // 2 + 1)
        pick_src = jax.random.randint(salts[2], (), 0, groups)
        pick_dst = jax.random.randint(salts[3], (), 0, groups)
        counts = counts.at[pick_src, pick_dst].set(CAP)
        src_orders = jax.vmap(lambda sub: jax.random.permutation(sub, VIS_DEV))(jax.random.split(salts[4], groups))
        dst_orders = jax.vmap(lambda sub: jax.random.permutation(sub, DEC_DEV))(jax.random.split(salts[5], groups))
        src_offsets = jnp.cumsum(counts, axis=1) - counts
        dst_offsets = jnp.cumsum(counts, axis=0) - counts
        dst_ends = dst_offsets + counts
        totals = jnp.sum(counts, axis=0)
        slot_index = jnp.arange(DEC_DEV).astype(jnp.int32)
        sender = jnp.sum((dst_ends[:, :, None] <= slot_index[None, None, :]).astype(jnp.int32), axis=0)
        sender = jnp.minimum(sender, groups - 1)
        column = jnp.arange(groups).astype(jnp.int32)[:, None]
        offset_in = slot_index[None, :] - dst_offsets[sender, column]
        position_in = jnp.clip(src_offsets[sender, column] + offset_in, 0, VIS_DEV - 1)
        local_row = src_orders[sender, position_in]
        source = sender * VIS_DEV + local_row
        valid = slot_index[None, :] < totals[:, None]
        chosen = jnp.where(valid, source, VIS).astype(jnp.int32)
        where_to = column * DEC_DEV + dst_orders
        filled = jnp.full((DEC,), VIS, jnp.int32)
        return filled.at[where_to.reshape(-1)].set(chosen.reshape(-1))
    return jax.vmap(one_clip)(jax.random.split(key, CLIPS))


def block_levels(key, dims, shards, smallest, top_value):
    gain, own = 1.0, jax.random.fold_in(key, 6)
    for position, parts in shards:
        steps = jnp.exp(jax.random.uniform(jax.random.fold_in(own, position), (parts,), jnp.float32, smallest / len(shards), top_value / len(shards)))
        gain = gain * jnp.repeat(steps, dims[position] // parts).reshape([-1 if axis == position else 1 for axis in range(len(dims))])
    return gain


def gaussian(rng, shape, scale, bound, cuts=(), held_as=jnp.bfloat16):
    array = jax.random.normal(rng, shape, jnp.float32) * scale
    if len(cuts) > 0:
        array = block_levels(rng, shape, cuts, -0.22, 0.18) * array
    return jnp.clip(array, min=-bound, max=bound).astype(held_as)


def setup_inputs(seed: int = 0) -> dict:
    splits = jax.random.split(jax.random.key(seed), 10)
    return {
        "tokens": draw_tokens(jax.random.fold_in(splits[9], 71), 0),
        "slot_keys": draw_slot_keys(jax.random.fold_in(splits[9], 71), 0),
        "w_in": gaussian(splits[2], (EXPERTS, D, HID), D ** -0.5, 0.1875, ((0, 16), (2, 8))),
        "w_back": gaussian(splits[3], (EXPERTS, HID, D), HID ** -0.5, 0.09375, ((0, 16), (1, 8))),
        "w_proj": gaussian(splits[4], (D, DD), D ** -0.5, 0.1875),
        "dec_source": draw_dec_source(jax.random.fold_in(splits[9], 71), 0),
        "mask_token": draw_mask_token(jax.random.fold_in(splits[9], 71), 0),
        "w_qkv": draw_w_qkv(jax.random.fold_in(splits[9], 71), 0),
        "w_out": gaussian(splits[8], (DD, DD), 1.5, 9.0),
    }


def layer_norm(values):
    centre = values - lax.optimization_barrier(jnp.mean(values, axis=-1, keepdims=True))
    spread = lax.optimization_barrier(jnp.mean(centre * centre, axis=-1, keepdims=True))
    return centre * lax.rsqrt(spread + 1e-05)

def sinusoid(places, width):
    half = width // 2
    speeds = jnp.exp(-math.log(10000.0) * jnp.arange(half).astype(jnp.float32) / half)
    angles = places.astype(jnp.float32)[:, None] * speeds[None, :]
    return jnp.concatenate([jnp.sin(angles), jnp.cos(angles)], axis=1)

def attend(queries, key_rows, value_rows):
    heads_here, head_dim, count = queries.shape
    block = math.gcd(count, 512)
    scale = 1.0 / math.sqrt(head_dim)
    blocks = queries.reshape(heads_here, head_dim, count // block, block).transpose(2, 0, 1, 3)

    def one_block(query_block):
        scores = jnp.einsum('hkq,hkn->hqn', query_block.astype(jnp.float32), key_rows.astype(jnp.float32)) * scale
        highest = lax.optimization_barrier(jnp.max(scores, axis=-1))
        raised = jnp.exp(scores - highest[..., None]).astype(jnp.bfloat16)
        totals = lax.optimization_barrier(jnp.sum(raised.astype(jnp.float32), axis=-1))
        summed = jnp.einsum('hqn,hkn->hkq', raised.astype(jnp.float32), value_rows.astype(jnp.float32))
        return (summed / totals[:, None, :]).astype(jnp.bfloat16)
    outcome = lax.map(one_block, blocks)
    return outcome.transpose(1, 2, 0, 3).reshape(heads_here, head_dim, count)

def reference(tokens, slot_keys, w_in, w_back, w_proj, dec_source, mask_token, w_qkv, w_out):
    clip_tokens = tokens.reshape(CLIPS, VIS, D)

    def one_clip(inputs):
        clip_rows, listing = inputs
        normed = layer_norm(clip_rows.astype(jnp.float32)).astype(jnp.bfloat16)
        logits = jnp.dot(normed.astype(jnp.float32), slot_keys.astype(jnp.float32), preferred_element_type=jnp.float32)
        col_top = lax.optimization_barrier(jnp.max(logits, axis=0))
        dispatch = jnp.exp(logits - col_top[None, :]).astype(jnp.bfloat16)
        slot_sums = jnp.dot(dispatch.T.astype(jnp.float32), normed.astype(jnp.float32), preferred_element_type=jnp.float32)
        slot_totals = lax.optimization_barrier(jnp.sum(dispatch.astype(jnp.float32), axis=0))
        slot_in = (slot_sums / slot_totals[:, None]).astype(jnp.bfloat16)

        def expert(inputs_e):
            rows_e, first, second = inputs_e
            hidden = jax.nn.gelu(jnp.dot(rows_e.astype(jnp.float32), first.astype(jnp.float32), preferred_element_type=jnp.float32)).astype(jnp.bfloat16)
            return jnp.dot(hidden.astype(jnp.float32), second.astype(jnp.float32), preferred_element_type=jnp.float32).astype(jnp.bfloat16)
        slot_out = lax.map(expert, (slot_in.reshape(EXPERTS, SLOTS_E, D), w_in, w_back)).reshape(SLOTS, D)
        row_top = lax.optimization_barrier(jnp.max(logits, axis=1, keepdims=True))
        raised = jnp.exp(logits - row_top)
        combine = (raised / lax.optimization_barrier(jnp.sum(raised, axis=1, keepdims=True))).astype(jnp.bfloat16)
        moe = jnp.dot(combine.astype(jnp.float32), slot_out.astype(jnp.float32), preferred_element_type=jnp.float32).astype(jnp.bfloat16)
        projected = jnp.dot(moe.astype(jnp.float32), w_proj.astype(jnp.float32), preferred_element_type=jnp.float32).astype(jnp.bfloat16)
        places = jnp.arange(DEC).astype(jnp.int32)
        filler = (mask_token.astype(jnp.float32)[None, :] + sinusoid(places, DD)).astype(jnp.bfloat16)
        visible = listing < VIS
        picked = jnp.take(projected, jnp.minimum(listing, VIS - 1).astype(jnp.int32), axis=0)
        dec_in = jnp.where(visible[:, None], picked, filler)
        dec_normed = layer_norm(dec_in.astype(jnp.float32)).astype(jnp.bfloat16)
        qkv = jnp.einsum('pd,dchk->chkp', dec_normed.astype(jnp.float32), w_qkv.reshape(DD, 3, HEADS, HD).astype(jnp.float32)).astype(jnp.bfloat16)
        attended = attend(qkv[0], qkv[1], qkv[2])
        mixed = jnp.einsum('hkp,hke->pe', attended.astype(jnp.float32), w_out.reshape(HEADS, HD, DD).astype(jnp.float32))
        return (mixed + dec_in.astype(jnp.float32)).astype(jnp.bfloat16)
    decoded = lax.map(one_clip, (clip_tokens, dec_source))
    return decoded.reshape(CLIPS * DEC, DD)
```

```python
import functools
import math

import jax
import jax.numpy as jnp
import numpy as np
from jax import lax
from jax.experimental import pallas as pl
from jax.experimental.pallas import tpu as pltpu
from jax.sharding import PartitionSpec as P

MESH = pl.DeviceIdType.MESH
F32 = jnp.float32
BF16 = jnp.bfloat16
D = 1024
SL = 64
SLOTS = 1024
DD = 512
VIS = 512
POS = 256
CAP = 16
HEADS = 16
HD = 32
HID = 512
R = 4
NT = 16
NC = 8
EXT = 128
KC = 512


def dot(a, b, ca=1, cb=0):
    return lax.dot_general(a, b, (((ca,), (cb,)), ((), ())), preferred_element_type=F32)


def layer_norm(v):
    centre = v - jnp.mean(v, axis=-1, keepdims=True)
    spread = jnp.mean(centre * centre, axis=-1, keepdims=True)
    return centre * lax.rsqrt(spread + 1e-05)


def iota(shape, dim):
    return lax.broadcasted_iota(jnp.int32, shape, dim)


def kernel(
    tokens_h, keys_h, w_in_h, w_back_h, w_proj_h, src_ref, mask_ref, w_qkv_h, w_out_h, freq_ref,
    out_ref,
    tokens, keys, w_in, w_back, w_proj, w_qkv, w_out,
    normed, logits, w_bp, w_qkvt, ranks,
    send_e, recv_e, combine, filler, dec_in,
    m_send, m_recv,
    s_y, r_y, s_z, r_z, s_y2, r_y2, s_z2, r_z2,
    ag_b, part_c, recv_c, ag_d, send_f, recv_f,
    k_rows, v_ext, sc0, sc1, att, recv_g,
    load_sem, e_s, e_r, m_s, m_r, a1_s, a1_r, a2_s, a2_r, b_s, b_r, c_s, c_r, d_s, d_r, f_s, f_r, g_s, g_r,
):
    c = lax.axis_index("clip")
    t = lax.axis_index("tok")
    x, co = c // 2, lax.rem(c, 2)
    y, z = t // R, lax.rem(t, R)

    def mod(v):
        return lax.rem(v, R)

    def rc(src, dst, ss, rs, dev):
        return pltpu.make_async_remote_copy(
            src_ref=src, dst_ref=dst, send_sem=ss, recv_sem=rs, device_id=dev, device_id_type=MESH
        )

    loads = {}
    for i, (name, h, v) in enumerate(
        (
            ("tokens", tokens_h, tokens), ("keys", keys_h, keys), ("w_proj", w_proj_h, w_proj),
            ("w_back", w_back_h, w_back), ("w_in", w_in_h, w_in), ("w_qkv", w_qkv_h, w_qkv),
            ("w_out", w_out_h, w_out),
        )
    ):
        loads[name] = pltpu.make_async_copy(h, v, load_sem.at[i])
        loads[name].start()

    offsets = [(dy, dz) for dy in range(R) for dz in range(R) if dy or dz]

    def tok_at(dy, dz):
        return mod(y + dy) * R + mod(z + dz)

    def clip_at(dx, f):
        return mod(x + dx) * 2 + (co if f == 0 else 1 - co)

    clip_offsets = [(0, 1)] + [(dx, f) for dx in (1, 3, 2) for f in (0, 1)]

    barrier = pltpu.get_barrier_semaphore()
    for dy, dz in offsets:
        pl.semaphore_signal(barrier, inc=1, device_id=(c, tok_at(dy, dz)), device_id_type=MESH)
    for dx, f in clip_offsets:
        pl.semaphore_signal(barrier, inc=1, device_id=(clip_at(dx, f), t), device_id_type=MESH)

    loads["tokens"].wait()
    for r in range(0, VIS, 128):
        normed[r : r + 128, 0:D] = layer_norm(tokens[r : r + 128, :].astype(F32)).astype(BF16)
    normed[:, D:] = jnp.ones((VIS, EXT), BF16)
    loads["keys"].wait()
    tops = []
    for k in range(4):
        part = dot(normed[:, 0:D], keys[:, k * 256 : (k + 1) * 256])
        logits[:, k * 256 : (k + 1) * 256] = part
        tops.append(jnp.max(part, axis=0, keepdims=True))
    for k in range(4):
        m_send[2 * k : 2 * k + 1, :] = tops[k][:, 0:128]
        m_send[2 * k + 1 : 2 * k + 2, :] = tops[k][:, 128:256]

    pl.semaphore_wait(barrier, len(offsets) + len(clip_offsets))
    m_cp = [
        rc(m_send, m_recv.at[i], m_s.at[i], m_r.at[i], (c, tok_at(dy, dz)))
        for i, (dy, dz) in enumerate(offsets)
    ]
    for cp in m_cp:
        cp.start()

    col = iota((1, POS), 1)
    for b in range(NT):
        mine = src_ref[:, b * POS : (b + 1) * POS]
        ranks[b : b + 1, :] = (lax.shift_right_logical(mine, 9) == t).astype(F32)
    before = (iota((POS, POS), 0) < iota((POS, POS), 1)).astype(F32).astype(BF16)
    ranks[NT:, :] = dot(ranks[0:NT, :].astype(BF16), before)
    for b in range(NT):
        mine = src_ref[:, b * POS : (b + 1) * POS]
        here = lax.shift_right_logical(mine, 9) == t
        code = jnp.where(here, ranks[NT + b : NT + b + 1, :].astype(jnp.int32), CAP)
        local = (mine & (VIS - 1)).astype(F32) + 1.0
        pick = jnp.where(code == iota((CAP, POS), 0), local, 0.0)
        row = jnp.sum(pick, axis=1, keepdims=True)
        onehot = (row == (iota((CAP, VIS), 1) + 1).astype(F32)).astype(F32).astype(BF16)
        send_e[b, :, 0:VIS] = onehot
    hot = send_e[:, :, 0:VIS].reshape(NT * CAP, VIS)
    rows = dot(hot, normed[:, 0:D]).astype(BF16)
    send_e[...] = rows.reshape(NT, CAP, D)
    recv_e[pl.ds(t, 1)] = send_e[pl.ds(t, 1)]
    e_cp = [
        rc(send_e.at[tok_at(dy, dz)], recv_e.at[t], e_s.at[i], e_r.at[i], (c, tok_at(dy, dz)))
        for i, (dy, dz) in enumerate(offsets)
    ]
    for cp in e_cp:
        cp.start()

    top8 = m_send[...]
    for i, cp in enumerate(m_cp):
        cp.wait_recv()
    for i in range(len(m_cp)):
        top8 = jnp.maximum(top8, m_recv[i])
    m_send_done = m_cp
    for cp in m_send_done:
        cp.wait_send()
    m_send[...] = top8

    y1, z1 = [], []
    for d in (1, 3, 2, 0):
        yy = mod(y + d)
        lanes = pl.ds(pl.multiple_of(yy * 256, 256), 256)
        pair = m_send[pl.ds(yy * 2, 2), :]
        top = jnp.concatenate([pair[0:1, :], pair[1:2, :]], axis=1)
        disp = jnp.exp(logits[:, lanes] - top).astype(BF16)
        sums = dot(disp, normed[...], 0, 0)
        s_y[pl.ds(yy, 1), :, 0:512] = sums[:, 0:512].astype(BF16)[None]
        s_y[pl.ds(yy, 1), :, 512:] = sums[:, D:].astype(BF16)[None]
        s_z[pl.ds(yy, 1)] = sums[:, 512:D].astype(BF16).reshape(1, R, SL, 512)
        if d:
            cp = rc(s_y.at[yy], r_y.at[d - 1], a1_s.at[d - 1], a1_r.at[d - 1], (c, tok_at(d, 0)))
            cp.start()
            y1.append(cp)
    for d in (1, 3, 2):
        zz = mod(z + d)
        cp = rc(s_z.at[:, zz], r_z.at[d - 1], a1_s.at[2 + d], a1_r.at[2 + d], (c, tok_at(0, d)))
        cp.start()
        z1.append(cp)

    loads["w_proj"].wait()
    loads["w_back"].wait()
    w_bp[...] = dot(w_back[...], w_proj[...]).astype(BF16)
    loads["w_qkv"].wait()
    for k in range(3):
        w_qkvt[k * DD : (k + 1) * DD, :] = w_qkv[:, k * DD : (k + 1) * DD].T
    place = (iota((POS, 1), 0) + t * POS).astype(F32)
    angle = place * freq_ref[...]
    mask = mask_ref[...].astype(F32)
    filler[:, 0:256] = (mask[:, 0:256] + jnp.sin(angle)).astype(BF16)
    filler[:, 256:512] = (mask[:, 256:512] + jnp.cos(angle)).astype(BF16)

    for cp in y1:
        cp.wait_recv()
    y2, own_y = [], None
    for d in (1, 3, 2, 0):
        at = pl.ds(pl.multiple_of(mod(z + d) * SL, SL), SL)
        total = s_y[pl.ds(y, 1), at, :].astype(F32)[0]
        for i in range(3):
            total = total + r_y[i, at, :].astype(F32)
        if d:
            s_y2[d - 1] = total.astype(BF16)
            cp = rc(s_y2.at[d - 1], r_y2.at[d - 1], a2_s.at[d - 1], a2_r.at[d - 1], (c, tok_at(0, d)))
            cp.start()
            y2.append(cp)
        else:
            own_y = total
    for cp in z1:
        cp.wait_recv()
    z2, own_z = [], None
    for d in (1, 3, 2, 0):
        yy = mod(y + d)
        total = s_z[pl.ds(yy, 1), pl.ds(z, 1)].astype(F32)[0, 0]
        for i in range(3):
            total = total + r_z[i, pl.ds(yy, 1)].astype(F32)[0]
        if d:
            s_z2[d - 1] = total.astype(BF16)
            cp = rc(s_z2.at[d - 1], r_z2.at[d - 1], a2_s.at[2 + d], a2_r.at[2 + d], (c, tok_at(d, 0)))
            cp.start()
            z2.append(cp)
        else:
            own_z = total

    for cp in e_cp:
        cp.wait_recv()
    got = recv_e[...].reshape(NT * CAP, D)
    lg = dot(got, keys[...])
    raised = jnp.exp(lg - jnp.max(lg, axis=1, keepdims=True))
    comb = (raised / jnp.sum(raised, axis=1, keepdims=True)).astype(BF16)
    own_row = src_ref[:, pl.ds(pl.multiple_of(t * POS, POS), POS)]
    block_row = lax.shift_right_logical(own_row, 9)
    square0, square1 = iota((POS, POS), 0), iota((POS, POS), 1)
    block_col = jnp.sum(
        jnp.where(square0 == square1, block_row.astype(F32), 0.0), axis=1, keepdims=True
    )
    same = (block_col == block_row.astype(F32)) & (square1 < square0)
    rank_col = jnp.sum(jnp.where(same, 1.0, 0.0), axis=1, keepdims=True)
    target = block_col * CAP + rank_col
    target = jnp.where(block_col >= NT, -1.0, target)
    place_hot = (target == square1.astype(F32)).astype(F32).astype(BF16)
    combine[...] = dot(place_hot, comb).astype(BF16)

    for cp in y2 + z2:
        cp.wait_recv()
    for i in range(3):
        own_y = own_y + r_y2[i].astype(F32)
        own_z = own_z + r_z2[i].astype(F32)
    inverse = 1.0 / own_y[:, 512:513]
    ag_b[pl.ds(c, 1), :, 0:512] = (own_y[:, 0:512] * inverse).astype(BF16)[None]
    ag_b[pl.ds(c, 1), :, 512:] = (own_z * inverse).astype(BF16)[None]

    b_cp = {}
    for dx in (1, 3, 2):
        b_cp[dx] = rc(ag_b.at[c], ag_b.at[c], b_s.at[dx - 1], b_r.at[dx - 1], (clip_at(dx, 0), t))
        b_cp[dx].start()
    partner = (clip_at(0, 1), t)
    fw = {0: rc(ag_b.at[c], ag_b.at[c], b_s.at[3], b_r.at[3], partner)}
    fw[0].start()
    loads["w_in"].wait()
    c_cp = []
    for step, dx in enumerate((0, 1, 3, 2)):
        chip = mod(x + R - dx)
        if dx:
            b_cp[dx].wait_recv()
            held = ag_b.at[chip * 2 + co]
            fw[dx] = rc(held, held, b_s.at[3 + dx], b_r.at[3 + dx], partner)
            fw[dx].start()
        fw[dx].wait_recv()
        rows = ag_b[pl.ds(chip * 2, 2)].reshape(2 * SL, D)
        hidden = jax.nn.gelu(dot(rows, w_in[...])).astype(BF16)
        part_c[pl.ds(chip * 2, 2)] = dot(hidden, w_bp[...]).astype(BF16).reshape(2, SL, DD)
        for f in (0, 1):
            if dx == 0 and f == 0:
                continue
            i = ((R - dx) % R) * 2 + f - 1
            to = clip_at(R - dx, f)
            cp = rc(part_c.at[to], recv_c.at[i], c_s.at[i], c_r.at[i], (to, t))
            cp.start()
            c_cp.append(cp)

    for cp in c_cp:
        cp.wait_recv()
    total = part_c[pl.ds(c, 1)].astype(F32)[0]
    for i in range(NC - 1):
        total = total + recv_c[i].astype(F32)
    ag_d[pl.ds(y, 1), pl.ds(z, 1)] = total.astype(BF16).reshape(1, 1, SL, DD)

    lo, hi = pl.ds(0, 256), pl.ds(256, 256)
    d1y, d1z, d2 = {}, {}, []
    for d in (1, 3, 2):
        d1y[d] = rc(
            ag_d.at[y, z, :, lo], ag_d.at[y, z, :, lo], d_s.at[d - 1], d_r.at[d - 1], (c, tok_at(d, 0))
        )
        d1y[d].start()
        d1z[d] = rc(
            ag_d.at[y, z, :, hi], ag_d.at[y, z, :, hi], d_s.at[2 + d], d_r.at[2 + d], (c, tok_at(0, d))
        )
        d1z[d].start()
    for d in (0, 1, 3, 2):
        if d:
            d1y[d].wait_recv()
            d1z[d].wait_recv()
        ya, za = mod(y + R - d), mod(z + R - d)
        for e in (1, 3, 2):
            i = 6 + d * 6 + (e - 1) * 2
            cp = rc(ag_d.at[ya, z, :, lo], ag_d.at[ya, z, :, lo], d_s.at[i], d_r.at[i], (c, tok_at(0, e)))
            cp.start()
            d2.append(cp)
            cp = rc(
                ag_d.at[y, za, :, hi], ag_d.at[y, za, :, hi], d_s.at[i + 1], d_r.at[i + 1], (c, tok_at(e, 0))
            )
            cp.start()
            d2.append(cp)
    for cp in d2:
        cp.wait_recv()

    shown = dot(combine[...], ag_d[...].reshape(SLOTS, DD)).astype(BF16)
    visible = block_col < NT
    held = jnp.where(visible, shown.astype(F32), filler[...].astype(F32))
    dec_in[...] = held.astype(BF16)
    dec_normed = layer_norm(held).astype(BF16)
    scale = math.log2(math.e) / math.sqrt(HD)
    for k in range(3):
        part = dot(w_qkvt[k * DD : (k + 1) * DD, :], dec_normed, 1, 1)
        if k == 0:
            part = part * scale
        send_f[:, k * HD : (k + 1) * HD, :] = part.astype(BF16).reshape(HEADS, HD, POS)
    recv_f[pl.ds(t, 1)] = send_f[pl.ds(t, 1)]
    f_cp = [
        rc(send_f.at[tok_at(dy, dz)], recv_f.at[t], f_s.at[i], f_r.at[i], (c, tok_at(dy, dz)))
        for i, (dy, dz) in enumerate(offsets)
    ]
    for cp in f_cp:
        cp.start()
    v_ext[HD:, :] = jnp.where(iota((16, NT * POS), 0) == 0, 1.0, 0.0).astype(BF16)
    for cp in f_cp:
        cp.wait_recv()

    def gather_keys(s, _):
        at = pl.ds(pl.multiple_of(s * POS, POS), POS)
        k_rows[at, :] = recv_f[s, HD : 2 * HD, :].T
        v_ext[0:HD, at] = recv_f[s, 2 * HD :, :]
        return 0

    lax.fori_loop(0, NT, gather_keys, 0)

    def scores(block, into):
        q = recv_f[block, 0:HD, :]
        top = None
        for k in range(NT * POS // KC):
            s = dot(k_rows[k * KC : (k + 1) * KC, :], q)
            into[k * KC : (k + 1) * KC, :] = s
            m = jnp.max(s.reshape(KC // 8, 8, POS), axis=0)
            top = m if top is None else jnp.maximum(top, m)
        return jnp.max(top, axis=0, keepdims=True)

    def finish(block, held, top):
        acc = jnp.zeros((HD + 16, POS), F32)
        for k in range(NT * POS // KC):
            p = jnp.exp2(held[k * KC : (k + 1) * KC, :] - top).astype(BF16)
            acc = acc + dot(v_ext[:, k * KC : (k + 1) * KC], p)
        att[pl.ds(block, 1)] = (acc[0:HD] / acc[HD : HD + 1]).astype(BF16)[None]

    def g_copy(i, block):
        return rc(att.at[block], recv_g.at[t], g_s.at[i], g_r.at[i], (c, block))

    def send_block(i, block):
        @pl.when(i < NT - 1)
        def _():
            g_copy(i, block).start()

    def at_step(i):
        return lax.rem(t + 1 + i, NT)

    top0 = scores(at_step(0), sc0)

    def two(j, top0):
        i = 2 * j
        top1 = scores(at_step(i + 1), sc1)
        finish(at_step(i), sc0, top0)
        send_block(i, at_step(i))
        nxt = scores(at_step(lax.rem(i + 2, NT)), sc0)
        finish(at_step(i + 1), sc1, top1)
        send_block(i + 1, at_step(i + 1))
        return nxt

    lax.fori_loop(0, NT // 2, two, top0)
    recv_g[pl.ds(t, 1)] = att[pl.ds(t, 1)]
    loads["w_out"].wait()
    for i in range(NT - 1):
        g_copy(i, at_step(i)).wait_recv()
    mixed = dot(recv_g[...].reshape(DD, POS), w_out[...], 0, 0)
    out_ref[...] = (mixed + dec_in[...].astype(F32)).astype(BF16)

    for cp in e_cp + y1 + z1 + y2 + z2 + list(b_cp.values()) + list(fw.values()) + c_cp:
        cp.wait_send()
    for cp in list(d1y.values()) + list(d1z.values()) + d2 + f_cp:
        cp.wait_send()
    for i in range(NT - 1):
        g_copy(i, at_step(i)).wait_send()


def per_device(tokens, slot_keys, w_in, w_back, w_proj, dec_source, mask_token, w_qkv, w_out):
    freq = jnp.asarray(np.exp(-math.log(10000.0) * np.arange(DD // 2) / (DD // 2)).astype(np.float32))
    V = pltpu.VMEM
    dma = lambda n: pltpu.SemaphoreType.DMA((n,))
    hbm = pl.BlockSpec(memory_space=pl.ANY)
    vm = pl.BlockSpec(memory_space=pltpu.VMEM)
    return pl.pallas_call(
        kernel,
        out_shape=jax.ShapeDtypeStruct((POS, DD), BF16),
        in_specs=[hbm, hbm, hbm, hbm, hbm, vm, vm, hbm, hbm, vm],
        out_specs=vm,
        scratch_shapes=[
            V((VIS, D), BF16), V((D, SLOTS), BF16), V((D, HID), BF16), V((HID, D), BF16),
            V((D, DD), BF16), V((DD, 3 * DD), BF16), V((DD, DD), BF16),
            V((VIS, D + EXT), BF16), V((VIS, SLOTS), F32), V((HID, DD), BF16), V((3 * DD, DD), BF16),
            V((2 * NT, POS), F32),
            V((NT, CAP, D), BF16), V((NT, CAP, D), BF16), V((POS, SLOTS), BF16), V((POS, DD), BF16),
            V((POS, DD), BF16),
            V((8, 128), F32), V((NT - 1, 8, 128), F32),
            V((R, 256, 512 + EXT), BF16), V((3, 256, 512 + EXT), BF16),
            V((R, R, SL, 512), BF16), V((3, R, SL, 512), BF16),
            V((3, SL, 512 + EXT), BF16), V((3, SL, 512 + EXT), BF16),
            V((3, SL, 512), BF16), V((3, SL, 512), BF16),
            V((NC, SL, D), BF16), V((NC, SL, DD), BF16), V((NC - 1, SL, DD), BF16),
            V((R, R, SL, DD), BF16), V((HEADS, 3 * HD, POS), BF16), V((NT, 3 * HD, POS), BF16),
            V((NT * POS, HD), BF16), V((HD + 16, NT * POS), BF16),
            V((NT * POS, POS), F32), V((NT * POS, POS), F32),
            V((NT, HD, POS), BF16), V((HEADS, HD, POS), BF16),
            dma(7), dma(15), dma(15), dma(15), dma(15), dma(6), dma(6), dma(6), dma(6),
            dma(7), dma(7), dma(7), dma(7), dma(30), dma(30), dma(15), dma(15), dma(15), dma(15),
        ],
        compiler_params=pltpu.CompilerParams(
            collective_id=0, has_side_effects=True, vmem_limit_bytes=60 << 20
        ),
        name="moe_mae",
    )(
        tokens, slot_keys, w_in[0], w_back[0], w_proj, dec_source, mask_token[None], w_qkv, w_out, freq[None]
    )


def solution(mesh):
    placed = (
        P(("clip", "tok"), None),
        P(),
        P("tok", None, "clip"),
        P("tok", "clip", None),
        P(),
        P("clip", None),
        P(),
        P(),
        P(),
    )
    return jax.shard_map(
        per_device, mesh=mesh, in_specs=placed, out_specs=P(("clip", "tok"), None), check_vma=False
    )
```

```python
import functools
import math

import jax
import jax.numpy as jnp
import numpy as np
from jax import lax
from jax.experimental import pallas as pl
from jax.experimental.pallas import tpu as pltpu
from jax.sharding import PartitionSpec as P

MESH = pl.DeviceIdType.MESH
F32 = jnp.float32
BF16 = jnp.bfloat16
D = 1024
SL = 64
SLOTS = 1024
DD = 512
VIS = 512
POS = 256
CAP = 16
HEADS = 16
HD = 32
HID = 512
R = 4
NT = 16
NC = 8
EXT = 128
KC = 512


def dot(a, b, ca=1, cb=0):
    return lax.dot_general(a, b, (((ca,), (cb,)), ((), ())), preferred_element_type=F32)


def layer_norm(v):
    centre = v - jnp.mean(v, axis=-1, keepdims=True)
    spread = jnp.mean(centre * centre, axis=-1, keepdims=True)
    return centre * lax.rsqrt(spread + 1e-05)


def iota(shape, dim):
    return lax.broadcasted_iota(jnp.int32, shape, dim)


def kernel(
    tokens_h, keys_h, w_in_h, w_back_h, w_proj_h, src_ref, mask_ref, w_qkv_h, w_out_h, freq_ref,
    out_ref,
    tokens, keys, w_in, w_back, w_proj, w_qkv, w_out,
    normed, logits, w_bp, w_qkvt, ranks,
    send_e, recv_e, combine, filler, dec_in,
    m_send, m_recv,
    s_y, r_y, s_z, r_z, s_y2, r_y2, s_z2, r_z2,
    ag_b, part_c, recv_c, ag_d, send_f, recv_f,
    k_rows, v_ext, sc0, sc1, att, recv_g,
    load_sem, e_s, e_r, m_s, m_r, a1_s, a1_r, a2_s, a2_r, b_s, b_r, c_s, c_r, d_s, d_r, f_s, f_r, g_s, g_r, q_s, q_r,
):
    c = lax.axis_index("clip")
    t = lax.axis_index("tok")
    x, co = c // 2, lax.rem(c, 2)
    y, z = t // R, lax.rem(t, R)

    def mod(v):
        return lax.rem(v, R)

    def rc(src, dst, ss, rs, dev):
        return pltpu.make_async_remote_copy(
            src_ref=src, dst_ref=dst, send_sem=ss, recv_sem=rs, device_id=dev, device_id_type=MESH
        )

    loads = {}
    for i, (name, h, v) in enumerate(
        (
            ("tokens", tokens_h, tokens), ("keys", keys_h, keys), ("w_proj", w_proj_h, w_proj),
            ("w_back", w_back_h, w_back), ("w_in", w_in_h, w_in), ("w_qkv", w_qkv_h, w_qkv),
            ("w_out", w_out_h, w_out),
        )
    ):
        loads[name] = pltpu.make_async_copy(h, v, load_sem.at[i])
        loads[name].start()

    offsets = [(dy, dz) for dy in range(R) for dz in range(R) if dy or dz]

    def tok_at(dy, dz):
        return mod(y + dy) * R + mod(z + dz)

    def clip_at(dx, f):
        return mod(x + dx) * 2 + (co if f == 0 else 1 - co)

    clip_offsets = [(0, 1)] + [(dx, f) for dx in (1, 3, 2) for f in (0, 1)]

    barrier = pltpu.get_barrier_semaphore()
    for dy, dz in offsets:
        pl.semaphore_signal(barrier, inc=1, device_id=(c, tok_at(dy, dz)), device_id_type=MESH)
    for dx, f in clip_offsets:
        pl.semaphore_signal(barrier, inc=1, device_id=(clip_at(dx, f), t), device_id_type=MESH)

    loads["tokens"].wait()
    for r in range(0, VIS, 128):
        normed[r : r + 128, 0:D] = layer_norm(tokens[r : r + 128, :].astype(F32)).astype(BF16)
    normed[:, D:] = jnp.ones((VIS, EXT), BF16)
    loads["keys"].wait()
    tops = []
    for k in range(4):
        part = dot(normed[:, 0:D], keys[:, k * 256 : (k + 1) * 256])
        logits[:, k * 256 : (k + 1) * 256] = part
        tops.append(jnp.max(part, axis=0, keepdims=True))
    for k in range(4):
        m_send[2 * k : 2 * k + 1, :] = tops[k][:, 0:128]
        m_send[2 * k + 1 : 2 * k + 2, :] = tops[k][:, 128:256]

    pl.semaphore_wait(barrier, len(offsets) + len(clip_offsets))
    m_cp = [
        rc(m_send, m_recv.at[i], m_s.at[i], m_r.at[i], (c, tok_at(dy, dz)))
        for i, (dy, dz) in enumerate(offsets)
    ]
    for cp in m_cp:
        cp.start()

    col = iota((1, POS), 1)
    for b in range(NT):
        mine = src_ref[:, b * POS : (b + 1) * POS]
        ranks[b : b + 1, :] = (lax.shift_right_logical(mine, 9) == t).astype(F32)
    before = (iota((POS, POS), 0) < iota((POS, POS), 1)).astype(F32).astype(BF16)
    ranks[NT:, :] = dot(ranks[0:NT, :].astype(BF16), before)
    for b in range(NT):
        mine = src_ref[:, b * POS : (b + 1) * POS]
        here = lax.shift_right_logical(mine, 9) == t
        code = jnp.where(here, ranks[NT + b : NT + b + 1, :].astype(jnp.int32), CAP)
        local = (mine & (VIS - 1)).astype(F32) + 1.0
        pick = jnp.where(code == iota((CAP, POS), 0), local, 0.0)
        row = jnp.sum(pick, axis=1, keepdims=True)
        onehot = (row == (iota((CAP, VIS), 1) + 1).astype(F32)).astype(F32).astype(BF16)
        send_e[b, :, 0:VIS] = onehot
    hot = send_e[:, :, 0:VIS].reshape(NT * CAP, VIS)
    rows = dot(hot, normed[:, 0:D]).astype(BF16)
    send_e[...] = rows.reshape(NT, CAP, D)
    recv_e[pl.ds(t, 1)] = send_e[pl.ds(t, 1)]
    e_cp = [
        rc(send_e.at[tok_at(dy, dz)], recv_e.at[t], e_s.at[i], e_r.at[i], (c, tok_at(dy, dz)))
        for i, (dy, dz) in enumerate(offsets)
    ]

    top8 = m_send[...]
    for i, cp in enumerate(m_cp):
        cp.wait_recv()
    for i in range(len(m_cp)):
        top8 = jnp.maximum(top8, m_recv[i])
    m_send_done = m_cp
    for cp in m_send_done:
        cp.wait_send()
    m_send[...] = top8

    y1, z1 = [], []
    for d in (1, 3, 2, 0):
        yy = mod(y + d)
        lanes = pl.ds(pl.multiple_of(yy * 256, 256), 256)
        pair = m_send[pl.ds(yy * 2, 2), :]
        top = jnp.concatenate([pair[0:1, :], pair[1:2, :]], axis=1)
        disp = jnp.exp(logits[:, lanes] - top).astype(BF16)
        sums = dot(disp, normed[...], 0, 0)
        s_y[pl.ds(yy, 1), :, 0:512] = sums[:, 0:512].astype(BF16)[None]
        s_y[pl.ds(yy, 1), :, 512:] = sums[:, D:].astype(BF16)[None]
        s_z[pl.ds(yy, 1)] = sums[:, 512:D].astype(BF16).reshape(1, R, SL, 512)
        if d:
            cp = rc(s_y.at[yy], r_y.at[d - 1], a1_s.at[d - 1], a1_r.at[d - 1], (c, tok_at(d, 0)))
            cp.start()
            y1.append(cp)
    for d in (1, 3, 2):
        zz = mod(z + d)
        cp = rc(s_z.at[:, zz], r_z.at[d - 1], a1_s.at[2 + d], a1_r.at[2 + d], (c, tok_at(0, d)))
        cp.start()
        z1.append(cp)

    loads["w_proj"].wait()
    loads["w_back"].wait()
    w_bp[...] = dot(w_back[...], w_proj[...]).astype(BF16)
    loads["w_qkv"].wait()
    for k in range(3):
        w_qkvt[k * DD : (k + 1) * DD, :] = w_qkv[:, k * DD : (k + 1) * DD].T
    place = (iota((POS, 1), 0) + t * POS).astype(F32)
    angle = place * freq_ref[...]
    mask = mask_ref[...].astype(F32).reshape(1, DD)
    filler[:, 0:256] = (mask[:, 0:256] + jnp.sin(angle)).astype(BF16)
    filler[:, 256:512] = (mask[:, 256:512] + jnp.cos(angle)).astype(BF16)

    for cp in y1:
        cp.wait_recv()
    y2, own_y = [], None
    for d in (1, 3, 2, 0):
        at = pl.ds(pl.multiple_of(mod(z + d) * SL, SL), SL)
        total = s_y[pl.ds(y, 1), at, :].astype(F32)[0]
        for i in range(3):
            total = total + r_y[i, at, :].astype(F32)
        if d:
            s_y2[d - 1] = total.astype(BF16)
            cp = rc(s_y2.at[d - 1], r_y2.at[d - 1], a2_s.at[d - 1], a2_r.at[d - 1], (c, tok_at(0, d)))
            cp.start()
            y2.append(cp)
        else:
            own_y = total
    for cp in z1:
        cp.wait_recv()
    z2, own_z = [], None
    for d in (1, 3, 2, 0):
        yy = mod(y + d)
        total = s_z[pl.ds(yy, 1), pl.ds(z, 1)].astype(F32)[0, 0]
        for i in range(3):
            total = total + r_z[i, pl.ds(yy, 1)].astype(F32)[0]
        if d:
            s_z2[d - 1] = total.astype(BF16)
            cp = rc(s_z2.at[d - 1], r_z2.at[d - 1], a2_s.at[2 + d], a2_r.at[2 + d], (c, tok_at(d, 0)))
            cp.start()
            z2.append(cp)
        else:
            own_z = total

    for cp in y2 + z2:
        cp.wait_recv()
    for cp in e_cp:
        cp.start()
    for i in range(3):
        own_y = own_y + r_y2[i].astype(F32)
        own_z = own_z + r_z2[i].astype(F32)
    inverse = 1.0 / own_y[:, 512:513]
    ag_b[pl.ds(c, 1), :, 0:512] = (own_y[:, 0:512] * inverse).astype(BF16)[None]
    ag_b[pl.ds(c, 1), :, 512:] = (own_z * inverse).astype(BF16)[None]

    b_cp = {}
    for dx in (1, 3, 2):
        b_cp[dx] = rc(ag_b.at[c], ag_b.at[c], b_s.at[dx - 1], b_r.at[dx - 1], (clip_at(dx, 0), t))
        b_cp[dx].start()
    partner = (clip_at(0, 1), t)
    fw = {0: rc(ag_b.at[c], ag_b.at[c], b_s.at[3], b_r.at[3], partner)}
    fw[0].start()
    loads["w_in"].wait()
    c_cp = []
    for step, dx in enumerate((0, 1, 3, 2)):
        chip = mod(x + R - dx)
        if dx:
            b_cp[dx].wait_recv()
            held = ag_b.at[chip * 2 + co]
            fw[dx] = rc(held, held, b_s.at[3 + dx], b_r.at[3 + dx], partner)
            fw[dx].start()
        fw[dx].wait_recv()
        rows = ag_b[pl.ds(chip * 2, 2)].reshape(2 * SL, D)
        hidden = jax.nn.gelu(dot(rows, w_in[...])).astype(BF16)
        part_c[pl.ds(chip * 2, 2)] = dot(hidden, w_bp[...]).astype(BF16).reshape(2, SL, DD)
        for f in (0, 1):
            if dx == 0 and f == 0:
                continue
            i = ((R - dx) % R) * 2 + f - 1
            to = clip_at(R - dx, f)
            cp = rc(part_c.at[to], recv_c.at[i], c_s.at[i], c_r.at[i], (to, t))
            cp.start()
            c_cp.append(cp)

    for cp in e_cp:
        cp.wait_recv()
    got = recv_e[...].reshape(NT * CAP, D)
    lg = dot(got, keys[...])
    raised = jnp.exp(lg - jnp.max(lg, axis=1, keepdims=True))
    comb = (raised / jnp.sum(raised, axis=1, keepdims=True)).astype(BF16)
    own_row = src_ref[:, pl.ds(pl.multiple_of(t * POS, POS), POS)]
    block_row = lax.shift_right_logical(own_row, 9)
    square0, square1 = iota((POS, POS), 0), iota((POS, POS), 1)
    block_col = jnp.sum(
        jnp.where(square0 == square1, block_row.astype(F32), 0.0), axis=1, keepdims=True
    )
    same = (block_col == block_row.astype(F32)) & (square1 < square0)
    rank_col = jnp.sum(jnp.where(same, 1.0, 0.0), axis=1, keepdims=True)
    target = block_col * CAP + rank_col
    target = jnp.where(block_col >= NT, -1.0, target)
    place_hot = (target == square1.astype(F32)).astype(F32).astype(BF16)
    combine[...] = dot(place_hot, comb).astype(BF16)

    for cp in c_cp:
        cp.wait_recv()
    total = part_c[pl.ds(c, 1)].astype(F32)[0]
    for i in range(NC - 1):
        total = total + recv_c[i].astype(F32)
    ag_d[pl.ds(y, 1), pl.ds(z, 1)] = total.astype(BF16).reshape(1, 1, SL, DD)

    lo, hi = pl.ds(0, 256), pl.ds(256, 256)
    d1y, d1z, d2 = {}, {}, []
    for d in (1, 3, 2):
        d1y[d] = rc(
            ag_d.at[y, z, :, lo], ag_d.at[y, z, :, lo], d_s.at[d - 1], d_r.at[d - 1], (c, tok_at(d, 0))
        )
        d1y[d].start()
        d1z[d] = rc(
            ag_d.at[y, z, :, hi], ag_d.at[y, z, :, hi], d_s.at[2 + d], d_r.at[2 + d], (c, tok_at(0, d))
        )
        d1z[d].start()
    for d in (0, 1, 3, 2):
        if d:
            d1y[d].wait_recv()
            d1z[d].wait_recv()
        ya, za = mod(y + R - d), mod(z + R - d)
        for e in (1, 3, 2):
            i = 6 + d * 6 + (e - 1) * 2
            cp = rc(ag_d.at[ya, z, :, lo], ag_d.at[ya, z, :, lo], d_s.at[i], d_r.at[i], (c, tok_at(0, e)))
            cp.start()
            d2.append(cp)
            cp = rc(
                ag_d.at[y, za, :, hi], ag_d.at[y, za, :, hi], d_s.at[i + 1], d_r.at[i + 1], (c, tok_at(e, 0))
            )
            cp.start()
            d2.append(cp)
    for cp in d2:
        cp.wait_recv()

    shown = dot(combine[...], ag_d[...].reshape(SLOTS, DD)).astype(BF16)
    visible = block_col < NT
    held = jnp.where(visible, shown.astype(F32), filler[...].astype(F32))
    dec_in[...] = held.astype(BF16)
    dec_normed = layer_norm(held).astype(BF16)
    scale = math.log2(math.e) / math.sqrt(HD)
    for k in range(3):
        part = dot(w_qkvt[k * DD : (k + 1) * DD, :], dec_normed, 1, 1)
        if k == 0:
            part = part * scale
        send_f[:, k * HD : (k + 1) * HD, :] = part.astype(BF16).reshape(HEADS, HD, POS)
    recv_f[pl.ds(t, 1)] = send_f[pl.ds(t, 1)]
    f_cp = [
        rc(
            send_f.at[tok_at(dy, dz), HD:], recv_f.at[t, HD:], f_s.at[i], f_r.at[i], (c, tok_at(dy, dz))
        )
        for i, (dy, dz) in enumerate(offsets)
    ]
    for cp in f_cp:
        cp.start()

    def at_step(i):
        return lax.rem(t + 1 + i, NT)

    def q_copy(i):
        to = lax.rem(t + NT - 1 - i, NT)
        return rc(send_f.at[to, 0:HD], recv_f.at[t, 0:HD], q_s.at[i], q_r.at[i], (c, to))

    for i in range(NT - 1):
        q_copy(i).start()
    v_ext[HD:, :] = jnp.where(iota((16, NT * POS), 0) == 0, 1.0, 0.0).astype(BF16)
    for cp in f_cp:
        cp.wait_recv()

    def gather_keys(s, _):
        at = pl.ds(pl.multiple_of(s * POS, POS), POS)
        k_rows[at, :] = recv_f[s, HD : 2 * HD, :].T
        v_ext[0:HD, at] = recv_f[s, 2 * HD :, :]
        return 0

    lax.fori_loop(0, NT, gather_keys, 0)

    def scores(block, into):
        q = recv_f[block, 0:HD, :]
        top = None
        for k in range(NT * POS // KC):
            s = dot(k_rows[k * KC : (k + 1) * KC, :], q)
            into[k * KC : (k + 1) * KC, :] = s
            m = jnp.max(s.reshape(KC // 8, 8, POS), axis=0)
            top = m if top is None else jnp.maximum(top, m)
        return jnp.max(top, axis=0, keepdims=True)

    def finish(block, held, top):
        acc = jnp.zeros((HD + 16, POS), F32)
        for k in range(NT * POS // KC):
            p = jnp.exp2(held[k * KC : (k + 1) * KC, :] - top).astype(BF16)
            acc = acc + dot(v_ext[:, k * KC : (k + 1) * KC], p)
        att[pl.ds(block, 1)] = (acc[0:HD] / acc[HD : HD + 1]).astype(BF16)[None]

    def g_copy(i, block):
        return rc(att.at[block], recv_g.at[t], g_s.at[i], g_r.at[i], (c, block))

    def send_block(i, block):
        @pl.when(i < NT - 1)
        def _():
            g_copy(i, block).start()

    def await_q(i):
        @pl.when(i < NT - 1)
        def _():
            q_copy(i).wait_recv()

    await_q(0)
    top0 = scores(at_step(0), sc0)

    def two(j, top0):
        i = 2 * j
        await_q(i + 1)
        top1 = scores(at_step(i + 1), sc1)
        finish(at_step(i), sc0, top0)
        send_block(i, at_step(i))
        await_q(i + 2)
        nxt = scores(at_step(lax.rem(i + 2, NT)), sc0)
        finish(at_step(i + 1), sc1, top1)
        send_block(i + 1, at_step(i + 1))
        return nxt

    lax.fori_loop(0, NT // 2, two, top0)
    recv_g[pl.ds(t, 1)] = att[pl.ds(t, 1)]
    loads["w_out"].wait()
    for i in range(NT - 1):
        g_copy(i, at_step(i)).wait_recv()
    mixed = dot(recv_g[...].reshape(DD, POS), w_out[...], 0, 0)
    out_ref[...] = (mixed + dec_in[...].astype(F32)).astype(BF16)

    for cp in e_cp + y1 + z1 + y2 + z2 + list(b_cp.values()) + list(fw.values()) + c_cp:
        cp.wait_send()
    for cp in list(d1y.values()) + list(d1z.values()) + d2 + f_cp:
        cp.wait_send()
    for i in range(NT - 1):
        g_copy(i, at_step(i)).wait_send()
        q_copy(i).wait_send()


def per_device(tokens, slot_keys, w_in, w_back, w_proj, dec_source, mask_token, w_qkv, w_out):
    freq = jnp.asarray(np.exp(-math.log(10000.0) * np.arange(DD // 2) / (DD // 2)).astype(np.float32))
    V = pltpu.VMEM
    dma = lambda n: pltpu.SemaphoreType.DMA((n,))
    hbm = pl.BlockSpec(memory_space=pl.ANY)
    vm = pl.BlockSpec(memory_space=pltpu.VMEM)
    return pl.pallas_call(
        kernel,
        out_shape=jax.ShapeDtypeStruct((POS, DD), BF16),
        in_specs=[hbm, hbm, hbm, hbm, hbm, vm, vm, hbm, hbm, vm],
        out_specs=vm,
        scratch_shapes=[
            V((VIS, D), BF16), V((D, SLOTS), BF16), V((D, HID), BF16), V((HID, D), BF16),
            V((D, DD), BF16), V((DD, 3 * DD), BF16), V((DD, DD), BF16),
            V((VIS, D + EXT), BF16), V((VIS, SLOTS), F32), V((HID, DD), BF16), V((3 * DD, DD), BF16),
            V((2 * NT, POS), F32),
            V((NT, CAP, D), BF16), V((NT, CAP, D), BF16), V((POS, SLOTS), BF16), V((POS, DD), BF16),
            V((POS, DD), BF16),
            V((8, 128), F32), V((NT - 1, 8, 128), F32),
            V((R, 256, 512 + EXT), BF16), V((3, 256, 512 + EXT), BF16),
            V((R, R, SL, 512), BF16), V((3, R, SL, 512), BF16),
            V((3, SL, 512 + EXT), BF16), V((3, SL, 512 + EXT), BF16),
            V((3, SL, 512), BF16), V((3, SL, 512), BF16),
            V((NC, SL, D), BF16), V((NC, SL, DD), BF16), V((NC - 1, SL, DD), BF16),
            V((R, R, SL, DD), BF16), V((HEADS, 3 * HD, POS), BF16), V((NT, 3 * HD, POS), BF16),
            V((NT * POS, HD), BF16), V((HD + 16, NT * POS), BF16),
            V((NT * POS, POS), F32), V((NT * POS, POS), F32),
            V((NT, HD, POS), BF16), V((HEADS, HD, POS), BF16),
            dma(7), dma(15), dma(15), dma(15), dma(15), dma(6), dma(6), dma(6), dma(6),
            dma(7), dma(7), dma(7), dma(7), dma(30), dma(30), dma(15), dma(15), dma(15), dma(15), dma(15), dma(15),
        ],
        compiler_params=pltpu.CompilerParams(
            collective_id=0, has_side_effects=True, vmem_limit_bytes=60 << 20
        ),
        name="moe_mae",
    )(
        tokens, slot_keys, w_in[0], w_back[0], w_proj, dec_source, mask_token, w_qkv, w_out, freq[None]
    )


def solution(mesh):
    placed = (
        P(("clip", "tok"), None),
        P(),
        P("tok", None, "clip"),
        P("tok", "clip", None),
        P(),
        P("clip", None),
        P(),
        P(),
        P(),
    )
    return jax.shard_map(
        per_device, mesh=mesh, in_specs=placed, out_specs=P(("clip", "tok"), None), check_vma=False
    )
```

```python
import functools
import math

import jax
import jax.numpy as jnp
import numpy as np
from jax import lax
from jax.experimental import pallas as pl
from jax.experimental.pallas import tpu as pltpu
from jax.sharding import PartitionSpec as P

MESH = pl.DeviceIdType.MESH
F32 = jnp.float32
BF16 = jnp.bfloat16
D = 1024
SL = 64
SLOTS = 1024
DD = 512
VIS = 512
POS = 256
CAP = 16
HEADS = 16
HD = 32
HID = 512
R = 4
NT = 16
NC = 8
KS = 512
KC = 512


def dot(a, b, ca=1, cb=0):
    return lax.dot_general(a, b, (((ca,), (cb,)), ((), ())), preferred_element_type=F32)


def layer_norm(v):
    centre = v - jnp.mean(v, axis=-1, keepdims=True)
    spread = jnp.mean(centre * centre, axis=-1, keepdims=True)
    return centre * lax.rsqrt(spread + 1e-05)


def iota(shape, dim):
    return lax.broadcasted_iota(jnp.int32, shape, dim)


def kernel(
    tokens_h, keys_h, w_in_h, w_back_h, w_proj_h, src_ref, mask_ref, w_qkv_h, w_out_h, freq_ref,
    out_ref,
    tokens, keys, w_in, w_back, w_proj, w_qkv, w_out,
    normed, disp, w_bp, w_qkvt, ranks,
    send_e, recv_e, combine, filler, dec_in,
    tops, weight,
    s_y, r_y, s_z, r_z, s_y2, r_y2, s_z2, r_z2,
    ag_b, part_c, recv_c, ag_d, send_f, recv_f,
    k_rows, v_ext, sc0, sc1, att, recv_g,
    load_sem, e_s, e_r, m_s, m_r, a1_s, a1_r, a2_s, a2_r, b_s, b_r, c_s, c_r, d_s, d_r, f_s, f_r, g_s, g_r, q_s, q_r,
):
    c = lax.axis_index("clip")
    t = lax.axis_index("tok")
    x, co = c // 2, lax.rem(c, 2)
    y, z = t // R, lax.rem(t, R)

    def mod(v):
        return lax.rem(v, R)

    def rc(src, dst, ss, rs, dev):
        return pltpu.make_async_remote_copy(
            src_ref=src, dst_ref=dst, send_sem=ss, recv_sem=rs, device_id=dev, device_id_type=MESH
        )

    loads = {}
    wanted = [(f"tokens{k}", tokens_h, tokens, (slice(k * 128, (k + 1) * 128),)) for k in range(4)]
    wanted += [
        ("keys", keys_h, keys, ()), ("w_proj", w_proj_h, w_proj, ()), ("w_back", w_back_h, w_back, ()), ("w_in", w_in_h, w_in, ()),
        ("w_qkv", w_qkv_h, w_qkv, ()), ("w_out", w_out_h, w_out, ()),
    ]
    for i, (name, h, v, at) in enumerate(wanted):
        loads[name] = pltpu.make_async_copy(h.at[at] if at else h, v.at[at] if at else v, load_sem.at[i])
        loads[name].start()

    offsets = [(dy, dz) for dy in range(R) for dz in range(R) if dy or dz]

    def tok_at(dy, dz):
        return mod(y + dy) * R + mod(z + dz)

    def clip_at(dx, f):
        return mod(x + dx) * 2 + (co if f == 0 else 1 - co)

    clip_offsets = [(0, 1)] + [(dx, f) for dx in (1, 3, 2) for f in (0, 1)]

    barrier = pltpu.get_barrier_semaphore()
    for dy, dz in offsets:
        pl.semaphore_signal(barrier, inc=1, device_id=(c, tok_at(dy, dz)), device_id_type=MESH)
    for dx, f in clip_offsets:
        pl.semaphore_signal(barrier, inc=1, device_id=(clip_at(dx, f), t), device_id_type=MESH)

    for k in range(4):
        loads[f"tokens{k}"].wait()
        at = slice(k * 128, (k + 1) * 128)
        normed[at, :] = layer_norm(tokens[at, :].astype(F32)).astype(BF16)
    loads["keys"].wait()
    for k in range(4):
        at = slice(k * 256, (k + 1) * 256)
        part = dot(normed[...], keys[:, at])
        top = jnp.max(part, axis=0, keepdims=True)
        raised = jnp.exp(part - top).astype(BF16)
        disp[:, at] = raised
        tops[0, 0:1, at] = top
        tops[0, 1:2, at] = jnp.sum(raised.astype(F32), axis=0, keepdims=True)

    pl.semaphore_wait(barrier, len(offsets) + len(clip_offsets))
    m_cp = [
        rc(tops.at[0], tops.at[i + 1], m_s.at[i], m_r.at[i], (c, tok_at(dy, dz)))
        for i, (dy, dz) in enumerate(offsets)
    ]
    for cp in m_cp:
        cp.start()

    y1, z1 = [], []
    for d in (1, 3, 2, 0):
        yy = mod(y + d)
        sums = dot(disp[:, pl.ds(pl.multiple_of(yy * 256, 256), 256)], normed[...], 0, 0)
        s_y[pl.ds(yy, 1)] = sums[:, 0:512].astype(BF16)[None]
        s_z[pl.ds(yy, 1)] = sums[:, 512:D].astype(BF16).reshape(1, R, SL, 512)
        if d:
            cp = rc(s_y.at[yy], r_y.at[d - 1], a1_s.at[d - 1], a1_r.at[d - 1], (c, tok_at(d, 0)))
            cp.start()
            y1.append(cp)
    for d in (1, 3, 2):
        zz = mod(z + d)
        cp = rc(s_z.at[:, zz], r_z.at[d - 1], a1_s.at[2 + d], a1_r.at[2 + d], (c, tok_at(0, d)))
        cp.start()
        z1.append(cp)

    col = iota((1, POS), 1)
    for b in range(NT):
        mine = src_ref[:, b * POS : (b + 1) * POS]
        ranks[b : b + 1, :] = (lax.shift_right_logical(mine, 9) == t).astype(F32)
    before = (iota((POS, POS), 0) < iota((POS, POS), 1)).astype(F32).astype(BF16)
    ranks[NT:, :] = dot(ranks[0:NT, :].astype(BF16), before)
    for b in range(NT):
        mine = src_ref[:, b * POS : (b + 1) * POS]
        here = lax.shift_right_logical(mine, 9) == t
        code = jnp.where(here, ranks[NT + b : NT + b + 1, :].astype(jnp.int32), CAP)
        local = (mine & (VIS - 1)).astype(F32) + 1.0
        pick = jnp.where(code == iota((CAP, POS), 0), local, 0.0)
        row = jnp.sum(pick, axis=1, keepdims=True)
        onehot = (row == (iota((CAP, VIS), 1) + 1).astype(F32)).astype(F32).astype(BF16)
        send_e[b, :, 0:VIS] = onehot
    hot = send_e[:, :, 0:VIS].reshape(NT * CAP, VIS)
    rows = dot(hot, normed[...]).astype(BF16)
    send_e[...] = rows.reshape(NT, CAP, D)
    recv_e[pl.ds(t, 1)] = send_e[pl.ds(t, 1)]
    e_cp = [
        rc(send_e.at[tok_at(dy, dz)], recv_e.at[t], e_s.at[i], e_r.at[i], (c, tok_at(dy, dz)))
        for i, (dy, dz) in enumerate(offsets)
    ]

    loads["w_proj"].wait()
    loads["w_back"].wait()
    w_bp[...] = dot(w_back[...], w_proj[...]).astype(BF16)
    loads["w_qkv"].wait()
    for k in range(3):
        w_qkvt[k * DD : (k + 1) * DD, :] = w_qkv[:, k * DD : (k + 1) * DD].T
    place = (iota((POS, 1), 0) + t * POS).astype(F32)
    angle = place * freq_ref[...]
    mask = mask_ref[...].astype(F32).reshape(1, DD)
    filler[:, 0:256] = (mask[:, 0:256] + jnp.sin(angle)).astype(BF16)
    filler[:, 256:512] = (mask[:, 256:512] + jnp.cos(angle)).astype(BF16)

    for cp in m_cp:
        cp.wait_recv()
    high = tops[:, 0, :]
    shift = jnp.exp(high - jnp.max(high, axis=0, keepdims=True))
    share = shift / jnp.sum(shift * tops[:, 1, :], axis=0, keepdims=True)
    for k in range(8):
        weight[k * 128 : (k + 1) * 128, :] = share[:, k * 128 : (k + 1) * 128].T

    def weigh(e, dy, dz):
        i = offsets.index((dy, dz)) + 1 if dy or dz else 0
        return weight[pl.ds(pl.multiple_of(e * SL, SL), SL), i : i + 1]

    for cp in y1:
        cp.wait_recv()
    y2, own_y = [], None
    for d in (1, 3, 2, 0):
        at = pl.ds(pl.multiple_of(mod(z + d) * SL, SL), SL)
        e = y * R + mod(z + d)
        total = weigh(e, 0, 0) * s_y[pl.ds(y, 1), at, :].astype(F32)[0]
        for i in range(3):
            total = total + weigh(e, i + 1, 0) * r_y[i, at, :].astype(F32)
        if d:
            s_y2[d - 1] = total.astype(BF16)
            cp = rc(s_y2.at[d - 1], r_y2.at[d - 1], a2_s.at[d - 1], a2_r.at[d - 1], (c, tok_at(0, d)))
            cp.start()
            y2.append(cp)
        else:
            own_y = total
    for cp in z1:
        cp.wait_recv()
    z2, own_z = [], None
    for d in (1, 3, 2, 0):
        yy = mod(y + d)
        e = yy * R + z
        total = weigh(e, 0, 0) * s_z[pl.ds(yy, 1), pl.ds(z, 1)].astype(F32)[0, 0]
        for i in range(3):
            total = total + weigh(e, 0, i + 1) * r_z[i, pl.ds(yy, 1)].astype(F32)[0]
        if d:
            s_z2[d - 1] = total.astype(BF16)
            cp = rc(s_z2.at[d - 1], r_z2.at[d - 1], a2_s.at[2 + d], a2_r.at[2 + d], (c, tok_at(d, 0)))
            cp.start()
            z2.append(cp)
        else:
            own_z = total

    for cp in y2 + z2:
        cp.wait_recv()
    for cp in e_cp:
        cp.start()
    for i in range(3):
        own_y = own_y + r_y2[i].astype(F32)
        own_z = own_z + r_z2[i].astype(F32)
    ag_b[pl.ds(c, 1), :, 0:512] = own_y.astype(BF16)[None]
    ag_b[pl.ds(c, 1), :, 512:] = own_z.astype(BF16)[None]

    b_cp = {}
    for dx in (1, 3, 2):
        b_cp[dx] = rc(ag_b.at[c], ag_b.at[c], b_s.at[dx - 1], b_r.at[dx - 1], (clip_at(dx, 0), t))
        b_cp[dx].start()
    partner = (clip_at(0, 1), t)
    fw = {0: rc(ag_b.at[c], ag_b.at[c], b_s.at[3], b_r.at[3], partner)}
    fw[0].start()
    loads["w_in"].wait()
    c_cp = []
    for step, dx in enumerate((0, 1, 3, 2)):
        chip = mod(x + R - dx)
        if dx:
            b_cp[dx].wait_recv()
            held = ag_b.at[chip * 2 + co]
            fw[dx] = rc(held, held, b_s.at[3 + dx], b_r.at[3 + dx], partner)
            fw[dx].start()
        fw[dx].wait_recv()
        rows = ag_b[pl.ds(chip * 2, 2)].reshape(2 * SL, D)
        hidden = jax.nn.gelu(dot(rows, w_in[...])).astype(BF16)
        part_c[pl.ds(chip * 2, 2)] = dot(hidden, w_bp[...]).astype(BF16).reshape(2, SL, DD)
        for f in (0, 1):
            if dx == 0 and f == 0:
                continue
            i = ((R - dx) % R) * 2 + f - 1
            to = clip_at(R - dx, f)
            cp = rc(part_c.at[to], recv_c.at[i], c_s.at[i], c_r.at[i], (to, t))
            cp.start()
            c_cp.append(cp)

    for cp in e_cp:
        cp.wait_recv()
    got = recv_e[...].reshape(NT * CAP, D)
    lg = dot(got, keys[...])
    raised = jnp.exp(lg - jnp.max(lg, axis=1, keepdims=True))
    comb = (raised / jnp.sum(raised, axis=1, keepdims=True)).astype(BF16)
    own_row = src_ref[:, pl.ds(pl.multiple_of(t * POS, POS), POS)]
    block_row = lax.shift_right_logical(own_row, 9)
    square0, square1 = iota((POS, POS), 0), iota((POS, POS), 1)
    block_col = jnp.sum(
        jnp.where(square0 == square1, block_row.astype(F32), 0.0), axis=1, keepdims=True
    )
    same = (block_col == block_row.astype(F32)) & (square1 < square0)
    rank_col = jnp.sum(jnp.where(same, 1.0, 0.0), axis=1, keepdims=True)
    target = block_col * CAP + rank_col
    target = jnp.where(block_col >= NT, -1.0, target)
    place_hot = (target == square1.astype(F32)).astype(F32).astype(BF16)
    combine[...] = dot(place_hot, comb).astype(BF16)

    for cp in c_cp:
        cp.wait_recv()
    total = part_c[pl.ds(c, 1)].astype(F32)[0]
    for i in range(NC - 1):
        total = total + recv_c[i].astype(F32)
    ag_d[pl.ds(y, 1), pl.ds(z, 1)] = total.astype(BF16).reshape(1, 1, SL, DD)

    lo, hi = pl.ds(0, 256), pl.ds(256, 256)
    d1y, d1z, d2 = {}, {}, []
    for d in (1, 3, 2):
        d1y[d] = rc(
            ag_d.at[y, z, :, lo], ag_d.at[y, z, :, lo], d_s.at[d - 1], d_r.at[d - 1], (c, tok_at(d, 0))
        )
        d1y[d].start()
        d1z[d] = rc(
            ag_d.at[y, z, :, hi], ag_d.at[y, z, :, hi], d_s.at[2 + d], d_r.at[2 + d], (c, tok_at(0, d))
        )
        d1z[d].start()
    for d in (0, 1, 3, 2):
        if d:
            d1y[d].wait_recv()
            d1z[d].wait_recv()
        ya, za = mod(y + R - d), mod(z + R - d)
        for e in (1, 3, 2):
            i = 6 + d * 6 + (e - 1) * 2
            cp = rc(ag_d.at[ya, z, :, lo], ag_d.at[ya, z, :, lo], d_s.at[i], d_r.at[i], (c, tok_at(0, e)))
            cp.start()
            d2.append(cp)
            cp = rc(
                ag_d.at[y, za, :, hi], ag_d.at[y, za, :, hi], d_s.at[i + 1], d_r.at[i + 1], (c, tok_at(e, 0))
            )
            cp.start()
            d2.append(cp)
    for cp in d2:
        cp.wait_recv()

    shown = dot(combine[...], ag_d[...].reshape(SLOTS, DD)).astype(BF16)
    visible = block_col < NT
    held = jnp.where(visible, shown.astype(F32), filler[...].astype(F32))
    dec_in[...] = held.astype(BF16)
    dec_normed = layer_norm(held).astype(BF16)
    scale = math.log2(math.e) / math.sqrt(HD)
    for k in range(3):
        part = dot(w_qkvt[k * DD : (k + 1) * DD, :], dec_normed, 1, 1)
        if k == 0:
            part = part * scale
        send_f[:, k * HD : (k + 1) * HD, :] = part.astype(BF16).reshape(HEADS, HD, POS)
    recv_f[pl.ds(t, 1)] = send_f[pl.ds(t, 1)]
    f_cp = [
        rc(
            send_f.at[tok_at(dy, dz), HD:], recv_f.at[t, HD:], f_s.at[i], f_r.at[i], (c, tok_at(dy, dz))
        )
        for i, (dy, dz) in enumerate(offsets)
    ]
    for cp in f_cp:
        cp.start()

    def at_step(i):
        return lax.rem(t + 1 + i, NT)

    def q_copy(i):
        to = lax.rem(t + NT - 1 - i, NT)
        return rc(send_f.at[to, 0:HD], recv_f.at[t, 0:HD], q_s.at[i], q_r.at[i], (c, to))

    for i in range(NT - 1):
        q_copy(i).start()
    v_ext[HD:, :] = jnp.where(iota((16, NT * POS), 0) == 0, 1.0, 0.0).astype(BF16)
    for cp in f_cp:
        cp.wait_recv()

    def gather_keys(s, _):
        at = pl.ds(pl.multiple_of(s * POS, POS), POS)
        k_rows[at, :] = recv_f[s, HD : 2 * HD, :].T
        v_ext[0:HD, at] = recv_f[s, 2 * HD :, :]
        return 0

    lax.fori_loop(0, NT, gather_keys, 0)

    def scores(block, into):
        q = recv_f[block, 0:HD, :]
        top = None
        for k in range(NT * POS // KS):
            s = dot(k_rows[k * KS : (k + 1) * KS, :], q)
            into[k * KS : (k + 1) * KS, :] = s
            m = jnp.max(s.reshape(KS // 8, 8, POS), axis=0)
            top = m if top is None else jnp.maximum(top, m)
        return jnp.max(top, axis=0, keepdims=True)

    def finish(block, held, top):
        acc = jnp.zeros((HD + 16, POS), F32)
        for k in range(NT * POS // KC):
            p = jnp.exp2((held[k * KC : (k + 1) * KC, :] - top).astype(BF16))
            acc = acc + dot(v_ext[:, k * KC : (k + 1) * KC], p)
        att[pl.ds(block, 1)] = (acc[0:HD] / acc[HD : HD + 1]).astype(BF16)[None]

    def g_copy(i, block):
        return rc(att.at[block], recv_g.at[t], g_s.at[i], g_r.at[i], (c, block))

    def send_block(i, block):
        @pl.when(i < NT - 1)
        def _():
            g_copy(i, block).start()

    def await_q(i):
        @pl.when(i < NT - 1)
        def _():
            q_copy(i).wait_recv()

    await_q(0)
    top0 = scores(at_step(0), sc0)

    def two(j, top0):
        i = 2 * j
        await_q(i + 1)
        top1 = scores(at_step(i + 1), sc1)
        finish(at_step(i), sc0, top0)
        send_block(i, at_step(i))
        await_q(i + 2)
        nxt = scores(at_step(lax.rem(i + 2, NT)), sc0)
        finish(at_step(i + 1), sc1, top1)
        send_block(i + 1, at_step(i + 1))
        return nxt

    lax.fori_loop(0, NT // 2, two, top0)
    recv_g[pl.ds(t, 1)] = att[pl.ds(t, 1)]
    loads["w_out"].wait()
    for i in range(NT - 1):
        g_copy(i, at_step(i)).wait_recv()
    mixed = dot(recv_g[...].reshape(DD, POS), w_out[...], 0, 0)
    out_ref[...] = (mixed + dec_in[...].astype(F32)).astype(BF16)

    for cp in m_cp + e_cp + y1 + z1 + y2 + z2 + list(b_cp.values()) + list(fw.values()) + c_cp:
        cp.wait_send()
    for cp in list(d1y.values()) + list(d1z.values()) + d2 + f_cp:
        cp.wait_send()
    for i in range(NT - 1):
        g_copy(i, at_step(i)).wait_send()
        q_copy(i).wait_send()


def per_device(tokens, slot_keys, w_in, w_back, w_proj, dec_source, mask_token, w_qkv, w_out):
    freq = jnp.asarray(np.exp(-math.log(10000.0) * np.arange(DD // 2) / (DD // 2)).astype(np.float32))
    V = pltpu.VMEM
    dma = lambda n: pltpu.SemaphoreType.DMA((n,))
    hbm = pl.BlockSpec(memory_space=pl.ANY)
    vm = pl.BlockSpec(memory_space=pltpu.VMEM)
    return pl.pallas_call(
        kernel,
        out_shape=jax.ShapeDtypeStruct((POS, DD), BF16),
        in_specs=[hbm, hbm, hbm, hbm, hbm, vm, vm, hbm, hbm, vm],
        out_specs=vm,
        scratch_shapes=[
            V((VIS, D), BF16), V((D, SLOTS), BF16), V((D, HID), BF16), V((HID, D), BF16),
            V((D, DD), BF16), V((DD, 3 * DD), BF16), V((DD, DD), BF16),
            V((VIS, D), BF16), V((VIS, SLOTS), BF16), V((HID, DD), BF16), V((3 * DD, DD), BF16),
            V((2 * NT, POS), F32),
            V((NT, CAP, D), BF16), V((NT, CAP, D), BF16), V((POS, SLOTS), BF16), V((POS, DD), BF16),
            V((POS, DD), BF16),
            V((NT, 2, SLOTS), F32), V((SLOTS, NT), F32),
            V((R, 256, 512), BF16), V((3, 256, 512), BF16),
            V((R, R, SL, 512), BF16), V((3, R, SL, 512), BF16),
            V((3, SL, 512), BF16), V((3, SL, 512), BF16),
            V((3, SL, 512), BF16), V((3, SL, 512), BF16),
            V((NC, SL, D), BF16), V((NC, SL, DD), BF16), V((NC - 1, SL, DD), BF16),
            V((R, R, SL, DD), BF16), V((HEADS, 3 * HD, POS), BF16), V((NT, 3 * HD, POS), BF16),
            V((NT * POS, HD), BF16), V((HD + 16, NT * POS), BF16),
            V((NT * POS, POS), F32), V((NT * POS, POS), F32),
            V((NT, HD, POS), BF16), V((HEADS, HD, POS), BF16),
            dma(10), dma(15), dma(15), dma(15), dma(15), dma(6), dma(6), dma(6), dma(6),
            dma(7), dma(7), dma(7), dma(7), dma(30), dma(30), dma(15), dma(15), dma(15), dma(15), dma(15), dma(15),
        ],
        compiler_params=pltpu.CompilerParams(
            collective_id=0, has_side_effects=True, vmem_limit_bytes=60 << 20
        ),
        name="moe_mae",
    )(
        tokens, slot_keys, w_in[0], w_back[0], w_proj, dec_source, mask_token, w_qkv, w_out, freq[None]
    )


def solution(mesh):
    placed = (
        P(("clip", "tok"), None),
        P(),
        P("tok", None, "clip"),
        P("tok", "clip", None),
        P(),
        P("clip", None),
        P(),
        P(),
        P(),
    )
    return jax.shard_map(
        per_device, mesh=mesh, in_specs=placed, out_specs=P(("clip", "tok"), None), check_vma=False
    )
```

```python
import functools
import math

import jax
import jax.numpy as jnp
import numpy as np
from jax import lax
from jax.experimental import pallas as pl
from jax.experimental.pallas import tpu as pltpu
from jax.sharding import PartitionSpec as P

MESH = pl.DeviceIdType.MESH
F32 = jnp.float32
BF16 = jnp.bfloat16
D = 1024
SL = 64
SLOTS = 1024
DD = 512
VIS = 512
POS = 256
CAP = 16
HEADS = 16
HD = 32
HID = 512
R = 4
NT = 16
NC = 8
KC = 256


def dot(a, b, ca=1, cb=0):
    return lax.dot_general(a, b, (((ca,), (cb,)), ((), ())), preferred_element_type=F32)


def layer_norm(v):
    centre = v - jnp.mean(v, axis=-1, keepdims=True)
    spread = jnp.mean(centre * centre, axis=-1, keepdims=True)
    return centre * lax.rsqrt(spread + 1e-05)


def iota(shape, dim):
    return lax.broadcasted_iota(jnp.int32, shape, dim)


def kernel(
    tokens_h, keys_h, w_in_h, w_back_h, w_proj_h, src_ref, mask_ref, w_qkv_h, w_out_h, freq_ref,
    out_ref,
    tokens, keys, w_in, w_back, w_proj, w_qkv, w_out,
    normed, disp, w_bp, w_qkvt, ranks,
    send_e, recv_e, combine, filler, dec_in,
    tops, weight,
    s_y, r_y, s_z, r_z, p_all, q_all, s_y2, r_y2, s_z2, r_z2,
    ag_b, part_c, recv_c, ag_d, send_f, recv_f,
    k_rows, v_ext, sc0, sc1, att, recv_g,
    load_sem, e_s, e_r, m_s, m_r, a1_s, a1_r, a2_s, a2_r, b_s, b_r, c_s, c_r, d_s, d_r, f_s, f_r, g_s, g_r, q_s, q_r,
):
    c = lax.axis_index("clip")
    t = lax.axis_index("tok")
    x, co = c // 2, lax.rem(c, 2)
    y, z = t // R, lax.rem(t, R)

    def mod(v):
        return lax.rem(v, R)

    def rc(src, dst, ss, rs, dev):
        return pltpu.make_async_remote_copy(
            src_ref=src, dst_ref=dst, send_sem=ss, recv_sem=rs, device_id=dev, device_id_type=MESH
        )

    loads = {}
    wanted = [(f"tokens{k}", tokens_h, tokens, (slice(k * 128, (k + 1) * 128),)) for k in range(4)]
    wanted += [
        ("keys", keys_h, keys, ()), ("w_proj", w_proj_h, w_proj, ()), ("w_back", w_back_h, w_back, ()), ("w_in", w_in_h, w_in, ()),
        ("w_qkv", w_qkv_h, w_qkv, ()), ("w_out", w_out_h, w_out, ()),
    ]
    for i, (name, h, v, at) in enumerate(wanted):
        loads[name] = pltpu.make_async_copy(h.at[at] if at else h, v.at[at] if at else v, load_sem.at[i])
        loads[name].start()

    offsets = [(dy, dz) for dy in (2, 1, 3, 0) for dz in (2, 1, 3, 0) if dy or dz]
    offsets.sort(key=lambda o: -min(o[0], R - o[0]) - min(o[1], R - o[1]))

    def tok_at(dy, dz):
        return mod(y + dy) * R + mod(z + dz)

    def clip_at(dx, f):
        return mod(x + dx) * 2 + (co if f == 0 else 1 - co)

    clip_offsets = [(0, 1)] + [(dx, f) for dx in (1, 3, 2) for f in (0, 1)]

    barrier = pltpu.get_barrier_semaphore()
    for dy, dz in offsets:
        pl.semaphore_signal(barrier, inc=1, device_id=(c, tok_at(dy, dz)), device_id_type=MESH)
    for dx, f in clip_offsets:
        pl.semaphore_signal(barrier, inc=1, device_id=(clip_at(dx, f), t), device_id_type=MESH)

    for k in range(4):
        loads[f"tokens{k}"].wait()
        at = slice(k * 128, (k + 1) * 128)
        normed[at, :] = layer_norm(tokens[at, :].astype(F32)).astype(BF16)
    loads["keys"].wait()
    for k in range(4):
        at = slice(k * 256, (k + 1) * 256)
        part = dot(normed[...], keys[:, at])
        top = jnp.max(part, axis=0, keepdims=True)
        raised = jnp.exp(part - top).astype(BF16)
        disp[:, at] = raised
        tops[0, 0:1, at] = top
        tops[0, 1:2, at] = jnp.sum(raised.astype(F32), axis=0, keepdims=True)

    pl.semaphore_wait(barrier, len(offsets) + len(clip_offsets))
    m_cp = [
        rc(tops.at[0], tops.at[i + 1], m_s.at[i], m_r.at[i], (c, tok_at(dy, dz)))
        for i, (dy, dz) in enumerate(offsets)
    ]
    for cp in m_cp:
        cp.start()

    lo, hi = pl.ds(0, 256), pl.ds(256, 256)
    one = {}
    for d in (2, 1, 3, 0):
        yy = mod(y + d)
        sums = dot(disp[:, pl.ds(pl.multiple_of(yy * 256, 256), 256)], normed[...], 0, 0)
        s_y[pl.ds(yy, 1)] = sums[:, 0:512].astype(BF16).reshape(1, R, SL, 512)
        s_z[pl.ds(yy, 1)] = sums[:, 512:D].astype(BF16).reshape(1, R, SL, 512)
        if d == 2:
            one["y_far_up"] = rc(s_y.at[yy, :, :, lo], r_y.at[0], a1_s.at[0], a1_r.at[0], (c, tok_at(1, 0)))
            one["y_far_dn"] = rc(s_y.at[yy, :, :, hi], r_y.at[1], a1_s.at[1], a1_r.at[1], (c, tok_at(3, 0)))
            one["y_far_up"].start()
            one["y_far_dn"].start()
        elif d == 1:
            one["y_up"] = rc(s_y.at[yy, :, :, hi], r_y.at[2], a1_s.at[2], a1_r.at[2], (c, tok_at(1, 0)))
            one["y_up"].start()
        elif d == 3:
            one["y_dn"] = rc(s_y.at[yy, :, :, lo], r_y.at[3], a1_s.at[3], a1_r.at[3], (c, tok_at(3, 0)))
            one["y_dn"].start()
    z_up, z_dn, z_far = mod(z + 1), mod(z + 3), mod(z + 2)
    one["z_far_up"] = rc(s_z.at[:, z_far, :, lo], r_z.at[0], a1_s.at[6], a1_r.at[6], (c, tok_at(0, 1)))
    one["z_far_dn"] = rc(s_z.at[:, z_far, :, hi], r_z.at[1], a1_s.at[7], a1_r.at[7], (c, tok_at(0, 3)))
    one["z_up"] = rc(s_z.at[:, z_up, :, hi], r_z.at[2], a1_s.at[8], a1_r.at[8], (c, tok_at(0, 1)))
    one["z_dn"] = rc(s_z.at[:, z_dn, :, lo], r_z.at[3], a1_s.at[9], a1_r.at[9], (c, tok_at(0, 3)))
    for name in ("z_far_up", "z_far_dn", "z_up", "z_dn"):
        one[name].start()

    col = iota((1, POS), 1)
    for b in range(NT):
        mine = src_ref[:, b * POS : (b + 1) * POS]
        ranks[b : b + 1, :] = (lax.shift_right_logical(mine, 9) == t).astype(F32)
    before = (iota((POS, POS), 0) < iota((POS, POS), 1)).astype(F32).astype(BF16)
    ranks[NT:, :] = dot(ranks[0:NT, :].astype(BF16), before)
    for b in range(NT):
        mine = src_ref[:, b * POS : (b + 1) * POS]
        here = lax.shift_right_logical(mine, 9) == t
        code = jnp.where(here, ranks[NT + b : NT + b + 1, :].astype(jnp.int32), CAP)
        local = (mine & (VIS - 1)).astype(F32) + 1.0
        pick = jnp.where(code == iota((CAP, POS), 0), local, 0.0)
        row = jnp.sum(pick, axis=1, keepdims=True)
        onehot = (row == (iota((CAP, VIS), 1) + 1).astype(F32)).astype(F32).astype(BF16)
        send_e[b, :, 0:VIS] = onehot
    hot = send_e[:, :, 0:VIS].reshape(NT * CAP, VIS)
    rows = dot(hot, normed[...]).astype(BF16)
    send_e[...] = rows.reshape(NT, CAP, D)
    recv_e[pl.ds(t, 1)] = send_e[pl.ds(t, 1)]
    e_cp = [
        rc(send_e.at[tok_at(dy, dz)], recv_e.at[t], e_s.at[i], e_r.at[i], (c, tok_at(dy, dz)))
        for i, (dy, dz) in enumerate(offsets)
    ]

    loads["w_proj"].wait()
    loads["w_back"].wait()
    w_bp[...] = dot(w_back[...], w_proj[...]).astype(BF16)
    loads["w_qkv"].wait()
    for k in range(3):
        w_qkvt[k * DD : (k + 1) * DD, :] = w_qkv[:, k * DD : (k + 1) * DD].T
    place = (iota((POS, 1), 0) + t * POS).astype(F32)
    angle = place * freq_ref[...]
    mask = mask_ref[...].astype(F32).reshape(1, DD)
    filler[:, 0:256] = (mask[:, 0:256] + jnp.sin(angle)).astype(BF16)
    filler[:, 256:512] = (mask[:, 256:512] + jnp.cos(angle)).astype(BF16)

    for cp in m_cp:
        cp.wait_recv()
    high = tops[:, 0, :]
    shift = jnp.exp(high - jnp.max(high, axis=0, keepdims=True))
    share = shift / jnp.sum(shift * tops[:, 1, :], axis=0, keepdims=True)
    for e in range(0, NT, 2):
        turned = share[:, e * SL : (e + 2) * SL].T
        weight[e // R, e % R] = turned[0:SL, :]
        weight[e // R, e % R + 1] = turned[SL:, :]

    def column(dy, dz):
        i = offsets.index((dy, dz)) + 1 if dy or dz else 0
        return slice(i, i + 1)

    up_y, dn_y = mod(y + 1), mod(y + 3)

    def relay(name, far, own, mine, theirs, out, i, dev):
        one[name].wait_recv()
        out[...] = (theirs * far[...].astype(F32) + mine * own.astype(F32)).astype(BF16)
        cp = rc(out, q_all.at[i], a1_s.at[i], a1_r.at[i], dev)
        cp.start()
        return cp

    def w_y(yy, dy):
        return weight[pl.ds(yy, 1), :, :, column(dy, 0)][0]

    def w_z(zz, dz):
        return weight[:, pl.ds(zz, 1), :, column(0, dz)][:, 0]

    one["y_q_up"] = relay(
        "y_far_up", r_y.at[0], s_y[pl.ds(up_y, 1), :, :, 0:256][0], w_y(up_y, 0), w_y(up_y, 1),
        p_all.at[0], 4, (c, tok_at(1, 0)),
    )
    one["y_q_dn"] = relay(
        "y_far_dn", r_y.at[1], s_y[pl.ds(dn_y, 1), :, :, 256:512][0], w_y(dn_y, 0), w_y(dn_y, 3),
        p_all.at[1], 5, (c, tok_at(3, 0)),
    )
    one["z_q_up"] = relay(
        "z_far_up", r_z.at[0], s_z[:, pl.ds(z_up, 1), :, 0:256][:, 0], w_z(z_up, 0), w_z(z_up, 1),
        p_all.at[2], 10, (c, tok_at(0, 1)),
    )
    one["z_q_dn"] = relay(
        "z_far_dn", r_z.at[1], s_z[:, pl.ds(z_dn, 1), :, 256:512][:, 0], w_z(z_dn, 0), w_z(z_dn, 3),
        p_all.at[3], 11, (c, tok_at(0, 3)),
    )

    for name in ("y_up", "y_dn", "y_q_up", "y_q_dn"):
        one[name].wait_recv()
    y2, own_y = [], None
    for d in (1, 3, 2, 0):
        zz = mod(z + d)
        w = weight[pl.ds(y, 1), pl.ds(zz, 1)][0, 0]
        own = s_y[pl.ds(y, 1), pl.ds(zz, 1)][0, 0].astype(F32) * w[:, 0:1]
        left = own[:, 0:256] + q_all[4, pl.ds(zz, 1)][0].astype(F32)
        left = left + w[:, column(3, 0)] * r_y[3, pl.ds(zz, 1)][0].astype(F32)
        right = own[:, 256:512] + q_all[5, pl.ds(zz, 1)][0].astype(F32)
        right = right + w[:, column(1, 0)] * r_y[2, pl.ds(zz, 1)][0].astype(F32)
        total = jnp.concatenate([left, right], axis=1)
        if d:
            s_y2[d - 1] = total.astype(BF16)
            cp = rc(s_y2.at[d - 1], r_y2.at[d - 1], a2_s.at[d - 1], a2_r.at[d - 1], (c, tok_at(0, d)))
            cp.start()
            y2.append(cp)
        else:
            own_y = total
    for name in ("z_up", "z_dn", "z_q_up", "z_q_dn"):
        one[name].wait_recv()
    z2, own_z = [], None
    for d in (1, 3, 2, 0):
        yy = mod(y + d)
        w = weight[pl.ds(yy, 1), pl.ds(z, 1)][0, 0]
        own = s_z[pl.ds(yy, 1), pl.ds(z, 1)][0, 0].astype(F32) * w[:, 0:1]
        left = own[:, 0:256] + q_all[10, pl.ds(yy, 1)][0].astype(F32)
        left = left + w[:, column(0, 3)] * r_z[3, pl.ds(yy, 1)][0].astype(F32)
        right = own[:, 256:512] + q_all[11, pl.ds(yy, 1)][0].astype(F32)
        right = right + w[:, column(0, 1)] * r_z[2, pl.ds(yy, 1)][0].astype(F32)
        total = jnp.concatenate([left, right], axis=1)
        if d:
            s_z2[d - 1] = total.astype(BF16)
            cp = rc(s_z2.at[d - 1], r_z2.at[d - 1], a2_s.at[2 + d], a2_r.at[2 + d], (c, tok_at(d, 0)))
            cp.start()
            z2.append(cp)
        else:
            own_z = total

    for cp in y2 + z2:
        cp.wait_recv()
    for cp in e_cp:
        cp.start()
    for i in range(3):
        own_y = own_y + r_y2[i].astype(F32)
        own_z = own_z + r_z2[i].astype(F32)
    ag_b[pl.ds(c, 1), :, 0:512] = own_y.astype(BF16)[None]
    ag_b[pl.ds(c, 1), :, 512:] = own_z.astype(BF16)[None]

    b_cp = {}
    for dx in (1, 3, 2):
        b_cp[dx] = rc(ag_b.at[c], ag_b.at[c], b_s.at[dx - 1], b_r.at[dx - 1], (clip_at(dx, 0), t))
        b_cp[dx].start()
    partner = (clip_at(0, 1), t)
    fw = {0: rc(ag_b.at[c], ag_b.at[c], b_s.at[3], b_r.at[3], partner)}
    fw[0].start()
    loads["w_in"].wait()
    c_cp = []
    for step, dx in enumerate((0, 1, 3, 2)):
        chip = mod(x + R - dx)
        if dx:
            b_cp[dx].wait_recv()
            held = ag_b.at[chip * 2 + co]
            fw[dx] = rc(held, held, b_s.at[3 + dx], b_r.at[3 + dx], partner)
            fw[dx].start()
        fw[dx].wait_recv()
        rows = ag_b[pl.ds(chip * 2, 2)].reshape(2 * SL, D)
        hidden = jax.nn.gelu(dot(rows, w_in[...])).astype(BF16)
        part_c[pl.ds(chip * 2, 2)] = dot(hidden, w_bp[...]).astype(BF16).reshape(2, SL, DD)
        for f in (0, 1):
            if dx == 0 and f == 0:
                continue
            i = ((R - dx) % R) * 2 + f - 1
            to = clip_at(R - dx, f)
            cp = rc(part_c.at[to], recv_c.at[i], c_s.at[i], c_r.at[i], (to, t))
            cp.start()
            c_cp.append(cp)

    for cp in e_cp:
        cp.wait_recv()
    got = recv_e[...].reshape(NT * CAP, D)
    lg = dot(got, keys[...])
    raised = jnp.exp(lg - jnp.max(lg, axis=1, keepdims=True))
    comb = (raised / jnp.sum(raised, axis=1, keepdims=True)).astype(BF16)
    own_row = src_ref[:, pl.ds(pl.multiple_of(t * POS, POS), POS)]
    block_row = lax.shift_right_logical(own_row, 9)
    square0, square1 = iota((POS, POS), 0), iota((POS, POS), 1)
    block_col = jnp.sum(
        jnp.where(square0 == square1, block_row.astype(F32), 0.0), axis=1, keepdims=True
    )
    same = (block_col == block_row.astype(F32)) & (square1 < square0)
    rank_col = jnp.sum(jnp.where(same, 1.0, 0.0), axis=1, keepdims=True)
    target = block_col * CAP + rank_col
    target = jnp.where(block_col >= NT, -1.0, target)
    place_hot = (target == square1.astype(F32)).astype(F32).astype(BF16)
    combine[...] = dot(place_hot, comb).astype(BF16)

    for cp in c_cp:
        cp.wait_recv()
    total = part_c[pl.ds(c, 1)].astype(F32)[0]
    for i in range(NC - 1):
        total = total + recv_c[i].astype(F32)
    ag_d[pl.ds(y, 1), pl.ds(z, 1)] = total.astype(BF16).reshape(1, 1, SL, DD)

    d1y, d1z, d2 = {}, {}, []
    for d in (1, 3, 2):
        d1y[d] = rc(
            ag_d.at[y, z, :, lo], ag_d.at[y, z, :, lo], d_s.at[d - 1], d_r.at[d - 1], (c, tok_at(d, 0))
        )
        d1y[d].start()
        d1z[d] = rc(
            ag_d.at[y, z, :, hi], ag_d.at[y, z, :, hi], d_s.at[2 + d], d_r.at[2 + d], (c, tok_at(0, d))
        )
        d1z[d].start()
    for d in (0, 1, 3, 2):
        if d:
            d1y[d].wait_recv()
            d1z[d].wait_recv()
        ya, za = mod(y + R - d), mod(z + R - d)
        for e in (1, 3, 2):
            i = 6 + d * 6 + (e - 1) * 2
            cp = rc(ag_d.at[ya, z, :, lo], ag_d.at[ya, z, :, lo], d_s.at[i], d_r.at[i], (c, tok_at(0, e)))
            cp.start()
            d2.append(cp)
            cp = rc(
                ag_d.at[y, za, :, hi], ag_d.at[y, za, :, hi], d_s.at[i + 1], d_r.at[i + 1], (c, tok_at(e, 0))
            )
            cp.start()
            d2.append(cp)
    for cp in d2:
        cp.wait_recv()

    shown = dot(combine[...], ag_d[...].reshape(SLOTS, DD)).astype(BF16)
    visible = block_col < NT
    held = jnp.where(visible, shown.astype(F32), filler[...].astype(F32))
    dec_in[...] = held.astype(BF16)
    dec_normed = layer_norm(held).astype(BF16)
    scale = math.log2(math.e) / math.sqrt(HD)
    for k in range(3):
        part = dot(w_qkvt[k * DD : (k + 1) * DD, :], dec_normed, 1, 1)
        if k == 0:
            part = part * scale
        send_f[:, k * HD : (k + 1) * HD, :] = part.astype(BF16).reshape(HEADS, HD, POS)
    recv_f[pl.ds(t, 1)] = send_f[pl.ds(t, 1)]
    f_cp = [
        rc(
            send_f.at[tok_at(dy, dz), HD:], recv_f.at[t, HD:], f_s.at[i], f_r.at[i], (c, tok_at(dy, dz))
        )
        for i, (dy, dz) in enumerate(offsets)
    ]
    for cp in f_cp:
        cp.start()

    def at_step(i):
        return lax.rem(t + 1 + i, NT)

    def q_copy(i):
        to = lax.rem(t + NT - 1 - i, NT)
        return rc(send_f.at[to, 0:HD], recv_f.at[t, 0:HD], q_s.at[i], q_r.at[i], (c, to))

    for i in range(NT - 1):
        q_copy(i).start()
    v_ext[HD:, :] = jnp.where(iota((16, NT * POS), 0) == 0, 1.0, 0.0).astype(BF16)
    for cp in f_cp:
        cp.wait_recv()

    def gather_keys(s, _):
        at = pl.ds(pl.multiple_of(s * POS, POS), POS)
        k_rows[at, :] = recv_f[s, HD : 2 * HD, :].T
        v_ext[0:HD, at] = recv_f[s, 2 * HD :, :]
        return 0

    lax.fori_loop(0, NT, gather_keys, 0)

    def turn(block, held, top, nxt, into):
        q = recv_f[nxt, 0:HD, :]
        acc, high = jnp.zeros((HD + 16, POS), F32), None
        for k in range(NT * POS // KC):
            at = slice(k * KC, (k + 1) * KC)
            if into is not None:
                s = dot(k_rows[at, :], q)
                into[at, :] = s
                m = jnp.max(s.reshape(KC // 8, 8, POS), axis=0)
                high = m if high is None else jnp.maximum(high, m)
            if held is not None:
                acc = acc + dot(v_ext[:, at], jnp.exp2((held[at, :] - top).astype(BF16)))
        if held is not None:
            att[pl.ds(block, 1)] = (acc[0:HD] / acc[HD : HD + 1]).astype(BF16)[None]
        return jnp.max(high, axis=0, keepdims=True)

    def g_copy(i, block):
        return rc(att.at[block], recv_g.at[t], g_s.at[i], g_r.at[i], (c, block))

    def send_block(i, block):
        @pl.when(i < NT - 1)
        def _():
            g_copy(i, block).start()

    def await_q(i):
        @pl.when(i < NT - 1)
        def _():
            q_copy(i).wait_recv()

    await_q(0)
    top0 = turn(None, None, None, at_step(0), sc0)

    def two(j, top0):
        i = 2 * j
        await_q(i + 1)
        top1 = turn(at_step(i), sc0, top0, at_step(i + 1), sc1)
        send_block(i, at_step(i))
        await_q(i + 2)
        nxt = turn(at_step(i + 1), sc1, top1, at_step(lax.rem(i + 2, NT)), sc0)
        send_block(i + 1, at_step(i + 1))
        return nxt

    lax.fori_loop(0, NT // 2, two, top0)
    recv_g[pl.ds(t, 1)] = att[pl.ds(t, 1)]
    loads["w_out"].wait()
    for i in range(NT - 1):
        g_copy(i, at_step(i)).wait_recv()
    mixed = dot(recv_g[...].reshape(DD, POS), w_out[...], 0, 0)
    out_ref[...] = (mixed + dec_in[...].astype(F32)).astype(BF16)

    for cp in m_cp + e_cp + list(one.values()) + y2 + z2 + list(b_cp.values()) + list(fw.values()) + c_cp:
        cp.wait_send()
    for cp in list(d1y.values()) + list(d1z.values()) + d2 + f_cp:
        cp.wait_send()
    for i in range(NT - 1):
        g_copy(i, at_step(i)).wait_send()
        q_copy(i).wait_send()


def per_device(tokens, slot_keys, w_in, w_back, w_proj, dec_source, mask_token, w_qkv, w_out):
    freq = jnp.asarray(np.exp(-math.log(10000.0) * np.arange(DD // 2) / (DD // 2)).astype(np.float32))
    V = pltpu.VMEM
    dma = lambda n: pltpu.SemaphoreType.DMA((n,))
    hbm = pl.BlockSpec(memory_space=pl.ANY)
    vm = pl.BlockSpec(memory_space=pltpu.VMEM)
    return pl.pallas_call(
        kernel,
        out_shape=jax.ShapeDtypeStruct((POS, DD), BF16),
        in_specs=[hbm, hbm, hbm, hbm, hbm, vm, vm, hbm, hbm, vm],
        out_specs=vm,
        scratch_shapes=[
            V((VIS, D), BF16), V((D, SLOTS), BF16), V((D, HID), BF16), V((HID, D), BF16),
            V((D, DD), BF16), V((DD, 3 * DD), BF16), V((DD, DD), BF16),
            V((VIS, D), BF16), V((VIS, SLOTS), BF16), V((HID, DD), BF16), V((3 * DD, DD), BF16),
            V((2 * NT, POS), F32),
            V((NT, CAP, D), BF16), V((NT, CAP, D), BF16), V((POS, SLOTS), BF16), V((POS, DD), BF16),
            V((POS, DD), BF16),
            V((NT, 2, SLOTS), F32), V((R, R, SL, NT), F32),
            V((R, R, SL, 512), BF16), V((4, R, SL, 256), BF16),
            V((R, R, SL, 512), BF16), V((4, R, SL, 256), BF16),
            V((4, R, SL, 256), BF16), V((12, R, SL, 256), BF16),
            V((3, SL, 512), BF16), V((3, SL, 512), BF16),
            V((3, SL, 512), BF16), V((3, SL, 512), BF16),
            V((NC, SL, D), BF16), V((NC, SL, DD), BF16), V((NC - 1, SL, DD), BF16),
            V((R, R, SL, DD), BF16), V((HEADS, 3 * HD, POS), BF16), V((NT, 3 * HD, POS), BF16),
            V((NT * POS, HD), BF16), V((HD + 16, NT * POS), BF16),
            V((NT * POS, POS), F32), V((NT * POS, POS), F32),
            V((NT, HD, POS), BF16), V((HEADS, HD, POS), BF16),
            dma(10), dma(15), dma(15), dma(15), dma(15), dma(12), dma(12), dma(6), dma(6),
            dma(7), dma(7), dma(7), dma(7), dma(30), dma(30), dma(15), dma(15), dma(15), dma(15), dma(15), dma(15),
        ],
        compiler_params=pltpu.CompilerParams(
            collective_id=0, has_side_effects=True, vmem_limit_bytes=60 << 20
        ),
        name="moe_mae",
    )(
        tokens, slot_keys, w_in[0], w_back[0], w_proj, dec_source, mask_token, w_qkv, w_out, freq[None]
    )


def solution(mesh):
    placed = (
        P(("clip", "tok"), None),
        P(),
        P("tok", None, "clip"),
        P("tok", "clip", None),
        P(),
        P("clip", None),
        P(),
        P(),
        P(),
    )
    return jax.shard_map(
        per_device, mesh=mesh, in_specs=placed, out_specs=P(("clip", "tok"), None), check_vma=False
    )
```

```python
import functools
import math

import jax
import jax.numpy as jnp
import numpy as np
from jax import lax
from jax.experimental import pallas as pl
from jax.experimental.pallas import tpu as pltpu
from jax.sharding import PartitionSpec as P

MESH = pl.DeviceIdType.MESH
F32 = jnp.float32
BF16 = jnp.bfloat16
D = 1024
SL = 64
SH = 32
SLOTS = 1024
DD = 512
VIS = 512
POS = 256
CAP = 16
HEADS = 16
HD = 32
HID = 512
R = 4
NT = 16
NC = 8
KC = 256


def dot(a, b, ca=1, cb=0):
    return lax.dot_general(a, b, (((ca,), (cb,)), ((), ())), preferred_element_type=F32)


def layer_norm(v):
    centre = v - jnp.mean(v, axis=-1, keepdims=True)
    spread = jnp.mean(centre * centre, axis=-1, keepdims=True)
    return centre * lax.rsqrt(spread + 1e-05)


def iota(shape, dim):
    return lax.broadcasted_iota(jnp.int32, shape, dim)


def kernel(
    tokens_h, keys_h, w_in_h, w_back_h, w_proj_h, src_ref, mask_ref, w_qkv_h, w_out_h, freq_ref,
    out_ref,
    tokens, keys, w_in, w_back, w_proj, w_qkv, w_out,
    normed, disp, w_bp, w_qkvt, ranks,
    send_e, recv_e, combine, filler, dec_in,
    tops, weight,
    s_y, r_y, s_z, r_z, p_all, q_all, s_y2, r_y2, s_z2, r_z2,
    ag_b, part_c, recv_c, ag_d, send_f, recv_f,
    k_rows, v_ext, sc0, sc1, att, recv_g,
    load_sem, e_s, e_r, m_s, m_r, a1_s, a1_r, a2_s, a2_r, b_s, b_r, c_s, c_r, d_s, d_r, f_s, f_r, g_s, g_r, q_s, q_r,
):
    c = lax.axis_index("clip")
    t = lax.axis_index("tok")
    x, co = c // 2, lax.rem(c, 2)
    y, z = t // R, lax.rem(t, R)

    def mod(v):
        return lax.rem(v, R)

    def rc(src, dst, ss, rs, dev):
        return pltpu.make_async_remote_copy(
            src_ref=src, dst_ref=dst, send_sem=ss, recv_sem=rs, device_id=dev, device_id_type=MESH
        )

    loads = {}
    wanted = [(f"tokens{k}", tokens_h, tokens, (slice(k * 128, (k + 1) * 128),)) for k in range(4)]
    wanted += [
        ("keys", keys_h, keys, ()), ("w_proj", w_proj_h, w_proj, ()), ("w_back", w_back_h, w_back, ()), ("w_in", w_in_h, w_in, ()),
        ("w_qkv", w_qkv_h, w_qkv, ()), ("w_out", w_out_h, w_out, ()),
    ]
    for i, (name, h, v, at) in enumerate(wanted):
        loads[name] = pltpu.make_async_copy(h.at[at] if at else h, v.at[at] if at else v, load_sem.at[i])
        loads[name].start()

    offsets = [(dy, dz) for dy in (2, 1, 3, 0) for dz in (2, 1, 3, 0) if dy or dz]
    offsets.sort(key=lambda o: -min(o[0], R - o[0]) - min(o[1], R - o[1]))

    def tok_at(dy, dz):
        return mod(y + dy) * R + mod(z + dz)

    def clip_at(dx, f):
        return mod(x + dx) * 2 + (co if f == 0 else 1 - co)

    clip_offsets = [(0, 1)] + [(dx, f) for dx in (1, 3, 2) for f in (0, 1)]

    barrier = pltpu.get_barrier_semaphore()
    for dy, dz in offsets:
        pl.semaphore_signal(barrier, inc=1, device_id=(c, tok_at(dy, dz)), device_id_type=MESH)
    for dx, f in clip_offsets:
        pl.semaphore_signal(barrier, inc=1, device_id=(clip_at(dx, f), t), device_id_type=MESH)

    for k in range(4):
        loads[f"tokens{k}"].wait()
        at = slice(k * 128, (k + 1) * 128)
        normed[at, :] = layer_norm(tokens[at, :].astype(F32)).astype(BF16)
    loads["keys"].wait()
    for k in range(4):
        at = slice(k * 256, (k + 1) * 256)
        part = dot(normed[...], keys[:, at])
        top = jnp.max(part, axis=0, keepdims=True)
        raised = jnp.exp(part - top).astype(BF16)
        disp[:, at] = raised
        tops[0, 0:1, at] = top
        tops[0, 1:2, at] = jnp.sum(raised.astype(F32), axis=0, keepdims=True)

    pl.semaphore_wait(barrier, len(offsets) + len(clip_offsets))
    m_cp = [
        rc(tops.at[0], tops.at[i + 1], m_s.at[i], m_r.at[i], (c, tok_at(dy, dz)))
        for i, (dy, dz) in enumerate(offsets)
    ]
    for cp in m_cp:
        cp.start()

    lo, hi = pl.ds(0, 256), pl.ds(256, 256)
    one = {}
    for d in (2, 1, 3, 0):
        yy = mod(y + d)
        sums = dot(disp[:, pl.ds(pl.multiple_of(yy * 256, 256), 256)], normed[...], 0, 0)
        s_y[pl.ds(yy, 1)] = sums[:, 0:512].astype(BF16).reshape(1, R, SL, 512)
        s_z[pl.ds(yy, 1)] = sums[:, 512:D].astype(BF16).reshape(1, R, SL, 512)
        if d == 2:
            one["y_far_up"] = rc(s_y.at[yy, :, :, lo], r_y.at[0], a1_s.at[0], a1_r.at[0], (c, tok_at(1, 0)))
            one["y_far_dn"] = rc(s_y.at[yy, :, :, hi], r_y.at[1], a1_s.at[1], a1_r.at[1], (c, tok_at(3, 0)))
            one["y_far_up"].start()
            one["y_far_dn"].start()
        elif d == 1:
            one["y_up"] = rc(s_y.at[yy, :, :, hi], r_y.at[2], a1_s.at[2], a1_r.at[2], (c, tok_at(1, 0)))
            one["y_up"].start()
        elif d == 3:
            one["y_dn"] = rc(s_y.at[yy, :, :, lo], r_y.at[3], a1_s.at[3], a1_r.at[3], (c, tok_at(3, 0)))
            one["y_dn"].start()
    z_up, z_dn, z_far = mod(z + 1), mod(z + 3), mod(z + 2)
    one["z_far_up"] = rc(s_z.at[:, z_far, :, lo], r_z.at[0], a1_s.at[6], a1_r.at[6], (c, tok_at(0, 1)))
    one["z_far_dn"] = rc(s_z.at[:, z_far, :, hi], r_z.at[1], a1_s.at[7], a1_r.at[7], (c, tok_at(0, 3)))
    one["z_up"] = rc(s_z.at[:, z_up, :, hi], r_z.at[2], a1_s.at[8], a1_r.at[8], (c, tok_at(0, 1)))
    one["z_dn"] = rc(s_z.at[:, z_dn, :, lo], r_z.at[3], a1_s.at[9], a1_r.at[9], (c, tok_at(0, 3)))
    for name in ("z_far_up", "z_far_dn", "z_up", "z_dn"):
        one[name].start()

    col = iota((1, POS), 1)
    for b in range(NT):
        mine = src_ref[:, b * POS : (b + 1) * POS]
        ranks[b : b + 1, :] = (lax.shift_right_logical(mine, 9) == t).astype(F32)
    before = (iota((POS, POS), 0) < iota((POS, POS), 1)).astype(F32).astype(BF16)
    ranks[NT:, :] = dot(ranks[0:NT, :].astype(BF16), before)
    for b in range(NT):
        mine = src_ref[:, b * POS : (b + 1) * POS]
        here = lax.shift_right_logical(mine, 9) == t
        code = jnp.where(here, ranks[NT + b : NT + b + 1, :].astype(jnp.int32), CAP)
        local = (mine & (VIS - 1)).astype(F32) + 1.0
        pick = jnp.where(code == iota((CAP, POS), 0), local, 0.0)
        row = jnp.sum(pick, axis=1, keepdims=True)
        onehot = (row == (iota((CAP, VIS), 1) + 1).astype(F32)).astype(F32).astype(BF16)
        send_e[b, :, 0:VIS] = onehot
    hot = send_e[:, :, 0:VIS].reshape(NT * CAP, VIS)
    rows = dot(hot, normed[...]).astype(BF16)
    send_e[...] = rows.reshape(NT, CAP, D)
    recv_e[pl.ds(t, 1)] = send_e[pl.ds(t, 1)]
    e_cp = [
        rc(send_e.at[tok_at(dy, dz)], recv_e.at[t], e_s.at[i], e_r.at[i], (c, tok_at(dy, dz)))
        for i, (dy, dz) in enumerate(offsets)
    ]

    loads["w_proj"].wait()
    loads["w_back"].wait()
    w_bp[...] = dot(w_back[...], w_proj[...]).astype(BF16)
    loads["w_qkv"].wait()
    for k in range(3):
        w_qkvt[k * DD : (k + 1) * DD, :] = w_qkv[:, k * DD : (k + 1) * DD].T
    place = (iota((POS, 1), 0) + t * POS).astype(F32)
    angle = place * freq_ref[...]
    mask = mask_ref[...].astype(F32).reshape(1, DD)
    filler[:, 0:256] = (mask[:, 0:256] + jnp.sin(angle)).astype(BF16)
    filler[:, 256:512] = (mask[:, 256:512] + jnp.cos(angle)).astype(BF16)

    for cp in m_cp:
        cp.wait_recv()
    high = tops[:, 0, :]
    shift = jnp.exp(high - jnp.max(high, axis=0, keepdims=True))
    share = shift / jnp.sum(shift * tops[:, 1, :], axis=0, keepdims=True)
    for e in range(0, NT, 2):
        turned = share[:, e * SL : (e + 2) * SL].T
        weight[e // R, e % R] = turned[0:SL, :]
        weight[e // R, e % R + 1] = turned[SL:, :]

    def column(dy, dz):
        i = offsets.index((dy, dz)) + 1 if dy or dz else 0
        return slice(i, i + 1)

    up_y, dn_y = mod(y + 1), mod(y + 3)

    def relay(name, far, own, mine, theirs, out, i, dev):
        one[name].wait_recv()
        out[...] = (theirs * far[...].astype(F32) + mine * own.astype(F32)).astype(BF16)
        cp = rc(out, q_all.at[i], a1_s.at[i], a1_r.at[i], dev)
        cp.start()
        return cp

    def w_y(yy, dy):
        return weight[pl.ds(yy, 1), :, :, column(dy, 0)][0]

    def w_z(zz, dz):
        return weight[:, pl.ds(zz, 1), :, column(0, dz)][:, 0]

    one["y_q_up"] = relay(
        "y_far_up", r_y.at[0], s_y[pl.ds(up_y, 1), :, :, 0:256][0], w_y(up_y, 0), w_y(up_y, 1),
        p_all.at[0], 4, (c, tok_at(1, 0)),
    )
    one["y_q_dn"] = relay(
        "y_far_dn", r_y.at[1], s_y[pl.ds(dn_y, 1), :, :, 256:512][0], w_y(dn_y, 0), w_y(dn_y, 3),
        p_all.at[1], 5, (c, tok_at(3, 0)),
    )
    one["z_q_up"] = relay(
        "z_far_up", r_z.at[0], s_z[:, pl.ds(z_up, 1), :, 0:256][:, 0], w_z(z_up, 0), w_z(z_up, 1),
        p_all.at[2], 10, (c, tok_at(0, 1)),
    )
    one["z_q_dn"] = relay(
        "z_far_dn", r_z.at[1], s_z[:, pl.ds(z_dn, 1), :, 256:512][:, 0], w_z(z_dn, 0), w_z(z_dn, 3),
        p_all.at[3], 11, (c, tok_at(0, 3)),
    )

    for name in ("y_up", "y_dn", "y_q_up", "y_q_dn"):
        one[name].wait_recv()
    def two(src, dst, i, h, base, dev):
        cp = rc(src.at[i, h], dst.at[i, h], a2_s.at[base + i], a2_r.at[base + i], dev)
        cp.start()
        return cp

    y2, own_y = [], None
    for d in (1, 3, 2, 0):
        zz = mod(z + d)
        w = weight[pl.ds(y, 1), pl.ds(zz, 1)][0, 0]
        own = s_y[pl.ds(y, 1), pl.ds(zz, 1)][0, 0].astype(F32) * w[:, 0:1]
        left = own[:, 0:256] + q_all[4, pl.ds(zz, 1)][0].astype(F32)
        left = left + w[:, column(3, 0)] * r_y[3, pl.ds(zz, 1)][0].astype(F32)
        right = own[:, 256:512] + q_all[5, pl.ds(zz, 1)][0].astype(F32)
        right = right + w[:, column(1, 0)] * r_y[2, pl.ds(zz, 1)][0].astype(F32)
        total = jnp.concatenate([left, right], axis=1)
        if d:
            s_y2[d - 1] = total.astype(BF16).reshape(2, SH, 512)
            y2.append(two(s_y2, r_y2, d - 1, 0, 0, (c, tok_at(0, d))))
        else:
            own_y = total
    for name in ("z_up", "z_dn", "z_q_up", "z_q_dn"):
        one[name].wait_recv()
    z2, own_z = [], None
    for d in (1, 3, 2, 0):
        yy = mod(y + d)
        w = weight[pl.ds(yy, 1), pl.ds(z, 1)][0, 0]
        own = s_z[pl.ds(yy, 1), pl.ds(z, 1)][0, 0].astype(F32) * w[:, 0:1]
        left = own[:, 0:256] + q_all[10, pl.ds(yy, 1)][0].astype(F32)
        left = left + w[:, column(0, 3)] * r_z[3, pl.ds(yy, 1)][0].astype(F32)
        right = own[:, 256:512] + q_all[11, pl.ds(yy, 1)][0].astype(F32)
        right = right + w[:, column(0, 1)] * r_z[2, pl.ds(yy, 1)][0].astype(F32)
        total = jnp.concatenate([left, right], axis=1)
        if d:
            s_z2[d - 1] = total.astype(BF16).reshape(2, SH, 512)
            z2.append(two(s_z2, r_z2, d - 1, 0, 3, (c, tok_at(d, 0))))
        else:
            own_z = total
    late = [two(s_y2, r_y2, d - 1, 1, 6, (c, tok_at(0, d))) for d in (1, 3, 2)]
    late += [two(s_z2, r_z2, d - 1, 1, 9, (c, tok_at(d, 0))) for d in (1, 3, 2)]
    second = [y2 + z2, late]

    b_cp, fw = {}, {}
    partner = (clip_at(0, 1), t)
    for h in (0, 1):
        for cp in second[h]:
            cp.wait_recv()
        at = slice(h * SH, (h + 1) * SH)
        left, right = own_y[at], own_z[at]
        for i in range(3):
            left = left + r_y2[i, h].astype(F32)
            right = right + r_z2[i, h].astype(F32)
        ag_b[h, pl.ds(c, 1), :, 0:512] = left.astype(BF16)[None]
        ag_b[h, pl.ds(c, 1), :, 512:] = right.astype(BF16)[None]
        held = ag_b.at[h, c]
        for dx in (1, 3, 2):
            i = h * 7 + dx - 1
            b_cp[h, dx] = rc(held, held, b_s.at[i], b_r.at[i], (clip_at(dx, 0), t))
            b_cp[h, dx].start()
        fw[h, 0] = rc(held, held, b_s.at[h * 7 + 3], b_r.at[h * 7 + 3], partner)
        fw[h, 0].start()
    for cp in e_cp:
        cp.start()
    loads["w_in"].wait()
    c_cp = [[], []]

    def hand_over(h):
        for dx in (1, 3, 2):
            b_cp[h, dx].wait_recv()
            held = ag_b.at[h, mod(x + R - dx) * 2 + co]
            i = h * 7 + 3 + dx
            fw[h, dx] = rc(held, held, b_s.at[i], b_r.at[i], partner)
            fw[h, dx].start()

    def expert(h, dx):
        chip = mod(x + R - dx)
        fw[h, dx].wait_recv()
        rows = ag_b[h, pl.ds(chip * 2, 2)].reshape(2 * SH, D)
        hidden = jax.nn.gelu(dot(rows, w_in[...])).astype(BF16)
        part_c[h, pl.ds(chip * 2, 2)] = dot(hidden, w_bp[...]).astype(BF16).reshape(2, SH, DD)
        for f in (0, 1):
            if dx == 0 and f == 0:
                continue
            i = ((R - dx) % R) * 2 + f - 1
            to = clip_at(R - dx, f)
            cp = rc(part_c.at[h, to], recv_c.at[h, i], c_s.at[h * 7 + i], c_r.at[h * 7 + i], (to, t))
            cp.start()
            c_cp[h].append(cp)

    expert(0, 0)
    expert(1, 0)
    hand_over(0)
    hand_over(1)
    for h in (0, 1):
        for dx in (1, 3, 2):
            expert(h, dx)

    for cp in e_cp:
        cp.wait_recv()
    got = recv_e[...].reshape(NT * CAP, D)
    lg = dot(got, keys[...])
    raised = jnp.exp(lg - jnp.max(lg, axis=1, keepdims=True))
    comb = (raised / jnp.sum(raised, axis=1, keepdims=True)).astype(BF16)
    own_row = src_ref[:, pl.ds(pl.multiple_of(t * POS, POS), POS)]
    block_row = lax.shift_right_logical(own_row, 9)
    square0, square1 = iota((POS, POS), 0), iota((POS, POS), 1)
    block_col = jnp.sum(
        jnp.where(square0 == square1, block_row.astype(F32), 0.0), axis=1, keepdims=True
    )
    same = (block_col == block_row.astype(F32)) & (square1 < square0)
    rank_col = jnp.sum(jnp.where(same, 1.0, 0.0), axis=1, keepdims=True)
    target = block_col * CAP + rank_col
    target = jnp.where(block_col >= NT, -1.0, target)
    place_hot = (target == square1.astype(F32)).astype(F32).astype(BF16)
    combine[...] = dot(place_hot, comb).astype(BF16)

    d1, d2 = {}, []

    def spread(h, key, src, dev):
        i = h * 30 + len([k for k in d1 if k[0] == h])
        d1[(h,) + key] = rc(src, src, d_s.at[i], d_r.at[i], dev)
        d1[(h,) + key].start()

    def onward(h, d):
        ya, za = mod(y + R - d), mod(z + R - d)
        for e in (1, 3, 2):
            spread(h, ("y", d, e), ag_d.at[ya, z, h, :, lo], (c, tok_at(0, e)))
            spread(h, ("z", d, e), ag_d.at[y, za, h, :, hi], (c, tok_at(e, 0)))

    for h in (0, 1):
        for cp in c_cp[h]:
            cp.wait_recv()
        total = part_c[h, pl.ds(c, 1)].astype(F32)[0]
        for i in range(NC - 1):
            total = total + recv_c[h, i].astype(F32)
        ag_d[pl.ds(y, 1), pl.ds(z, 1), h] = total.astype(BF16).reshape(1, 1, SH, DD)
        for d in (1, 3, 2):
            spread(h, ("y", d), ag_d.at[y, z, h, :, lo], (c, tok_at(d, 0)))
            spread(h, ("z", d), ag_d.at[y, z, h, :, hi], (c, tok_at(0, d)))
        onward(h, 0)
    for h in (0, 1):
        for d in (1, 3, 2):
            d1[h, "y", d].wait_recv()
            d1[h, "z", d].wait_recv()
            onward(h, d)
    d2 = [cp for key, cp in d1.items() if len(key) == 4]
    for cp in d2:
        cp.wait_recv()

    shown = dot(combine[...], ag_d[...].reshape(SLOTS, DD)).astype(BF16)
    visible = block_col < NT
    held = jnp.where(visible, shown.astype(F32), filler[...].astype(F32))
    dec_in[...] = held.astype(BF16)
    dec_normed = layer_norm(held).astype(BF16)
    scale = math.log2(math.e) / math.sqrt(HD)
    for k in (1, 2):
        part = dot(w_qkvt[k * DD : (k + 1) * DD, :], dec_normed, 1, 1)
        send_f[:, k * HD : (k + 1) * HD, :] = part.astype(BF16).reshape(HEADS, HD, POS)
    f_cp = [
        rc(
            send_f.at[tok_at(dy, dz), HD:], recv_f.at[t, HD:], f_s.at[i], f_r.at[i], (c, tok_at(dy, dz))
        )
        for i, (dy, dz) in enumerate(offsets)
    ]
    for cp in f_cp:
        cp.start()

    part = dot(w_qkvt[0:DD, :], dec_normed, 1, 1) * scale
    send_f[:, 0:HD, :] = part.astype(BF16).reshape(HEADS, HD, POS)
    recv_f[pl.ds(t, 1)] = send_f[pl.ds(t, 1)]

    def at_step(i):
        return lax.rem(t + 1 + i, NT)

    def q_copy(i):
        to = lax.rem(t + NT - 1 - i, NT)
        return rc(send_f.at[to, 0:HD], recv_f.at[t, 0:HD], q_s.at[i], q_r.at[i], (c, to))

    for i in range(NT - 1):
        q_copy(i).start()
    v_ext[HD:, :] = jnp.where(iota((16, NT * POS), 0) == 0, 1.0, 0.0).astype(BF16)
    for cp in f_cp:
        cp.wait_recv()

    for k in range(NT):
        at = slice(k * POS, (k + 1) * POS)
        k_rows[at, :] = recv_f[k, HD : 2 * HD, :].T
        v_ext[0:HD, at] = recv_f[k, 2 * HD :, :]

    def turn(block, held, top, nxt, into):
        q = None if into is None else recv_f[nxt, 0:HD, :]
        acc, high = jnp.zeros((HD + 16, POS), F32), None
        for k in range(NT * POS // KC):
            at = slice(k * KC, (k + 1) * KC)
            if into is not None:
                s = dot(k_rows[at, :], q)
                into[at, :] = s
                m = jnp.max(s.reshape(KC // 8, 8, POS), axis=0)
                high = m if high is None else jnp.maximum(high, m)
            if held is not None:
                acc = acc + dot(v_ext[:, at], jnp.exp2((held[at, :] - top).astype(BF16)))
        if held is not None:
            att[pl.ds(block, 1)] = (acc[0:HD] / acc[HD : HD + 1]).astype(BF16)[None]
        return None if high is None else jnp.max(high, axis=0, keepdims=True)

    def g_copy(i, block):
        return rc(att.at[block], recv_g.at[t], g_s.at[i], g_r.at[i], (c, block))

    q_copy(0).wait_recv()
    top0 = turn(None, None, None, at_step(0), sc0)

    def pair(j, top0):
        i = 2 * j
        q_copy(i + 1).wait_recv()
        top1 = turn(at_step(i), sc0, top0, at_step(i + 1), sc1)
        g_copy(i, at_step(i)).start()
        q_copy(i + 2).wait_recv()
        nxt = turn(at_step(i + 1), sc1, top1, at_step(i + 2), sc0)
        g_copy(i + 1, at_step(i + 1)).start()
        return nxt

    top0 = lax.fori_loop(0, NT // 2 - 1, pair, top0)
    top1 = turn(at_step(NT - 2), sc0, top0, at_step(NT - 1), sc1)
    g_copy(NT - 2, at_step(NT - 2)).start()
    turn(at_step(NT - 1), sc1, top1, None, None)
    recv_g[pl.ds(t, 1)] = att[pl.ds(t, 1)]
    loads["w_out"].wait()
    for i in range(NT - 1):
        g_copy(i, at_step(i)).wait_recv()
    mixed = dot(recv_g[...].reshape(DD, POS), w_out[...], 0, 0)
    out_ref[...] = (mixed + dec_in[...].astype(F32)).astype(BF16)

    for cp in m_cp + e_cp + list(one.values()) + second[0] + second[1] + list(b_cp.values()) + list(fw.values()) + c_cp[0] + c_cp[1]:
        cp.wait_send()
    for cp in list(d1.values()) + f_cp:
        cp.wait_send()
    for i in range(NT - 1):
        g_copy(i, at_step(i)).wait_send()
        q_copy(i).wait_send()


def per_device(tokens, slot_keys, w_in, w_back, w_proj, dec_source, mask_token, w_qkv, w_out):
    freq = jnp.asarray(np.exp(-math.log(10000.0) * np.arange(DD // 2) / (DD // 2)).astype(np.float32))
    V = pltpu.VMEM
    dma = lambda n: pltpu.SemaphoreType.DMA((n,))
    hbm = pl.BlockSpec(memory_space=pl.ANY)
    vm = pl.BlockSpec(memory_space=pltpu.VMEM)
    return pl.pallas_call(
        kernel,
        out_shape=jax.ShapeDtypeStruct((POS, DD), BF16),
        in_specs=[hbm, hbm, hbm, hbm, hbm, vm, vm, hbm, hbm, vm],
        out_specs=vm,
        scratch_shapes=[
            V((VIS, D), BF16), V((D, SLOTS), BF16), V((D, HID), BF16), V((HID, D), BF16),
            V((D, DD), BF16), V((DD, 3 * DD), BF16), V((DD, DD), BF16),
            V((VIS, D), BF16), V((VIS, SLOTS), BF16), V((HID, DD), BF16), V((3 * DD, DD), BF16),
            V((2 * NT, POS), F32),
            V((NT, CAP, D), BF16), V((NT, CAP, D), BF16), V((POS, SLOTS), BF16), V((POS, DD), BF16),
            V((POS, DD), BF16),
            V((NT, 2, SLOTS), F32), V((R, R, SL, NT), F32),
            V((R, R, SL, 512), BF16), V((4, R, SL, 256), BF16),
            V((R, R, SL, 512), BF16), V((4, R, SL, 256), BF16),
            V((4, R, SL, 256), BF16), V((12, R, SL, 256), BF16),
            V((3, 2, SH, 512), BF16), V((3, 2, SH, 512), BF16),
            V((3, 2, SH, 512), BF16), V((3, 2, SH, 512), BF16),
            V((2, NC, SH, D), BF16), V((2, NC, SH, DD), BF16), V((2, NC - 1, SH, DD), BF16),
            V((R, R, 2, SH, DD), BF16), V((HEADS, 3 * HD, POS), BF16), V((NT, 3 * HD, POS), BF16),
            V((NT * POS, HD), BF16), V((HD + 16, NT * POS), BF16),
            V((NT * POS, POS), F32), V((NT * POS, POS), F32),
            V((NT, HD, POS), BF16), V((HEADS, HD, POS), BF16),
            dma(10), dma(15), dma(15), dma(15), dma(15), dma(12), dma(12), dma(12), dma(12),
            dma(14), dma(14), dma(14), dma(14), dma(60), dma(60), dma(15), dma(15), dma(15), dma(15), dma(15), dma(15),
        ],
        compiler_params=pltpu.CompilerParams(
            collective_id=0, has_side_effects=True, vmem_limit_bytes=60 << 20
        ),
        name="moe_mae",
    )(
        tokens, slot_keys, w_in[0], w_back[0], w_proj, dec_source, mask_token, w_qkv, w_out, freq[None]
    )


def solution(mesh):
    placed = (
        P(("clip", "tok"), None),
        P(),
        P("tok", None, "clip"),
        P("tok", "clip", None),
        P(),
        P("clip", None),
        P(),
        P(),
        P(),
    )
    return jax.shard_map(
        per_device, mesh=mesh, in_specs=placed, out_specs=P(("clip", "tok"), None), check_vma=False
    )
```
